128 devices in a mesh: ctx: 8 (over x, core), head: 16 (over y, z).
Axes of the slice: x: 4, y: 4, z: 4, core: 2. Of those that a mesh axis runs over, the one named last changes fastest.
Arguments:
- queries: bfloat16 [16384, 8192], P(('ctx', 'head')), may hold values from -30 to 30
- keys: bfloat16 [16384, 8192], P(('ctx', 'head')), may hold values from -30 to 30
- values: bfloat16 [16384, 8192], P(('ctx', 'head')), may hold values from -6 to 6
- rates: bfloat16 [16384, 32], P(('ctx', 'head')), may hold values from 0.0009994507 to 0.0099487305
- fast_init: bfloat16 [3, 32, 256, 256], P(None, 'head'), may hold values from -0.375 to 0.375
- gain: float32 [8192], replicated, may hold values from 0.25 to 1.75
Outputs:
- mixed: bfloat16 [16384, 8192], P(('ctx', 'head'))
The draws below stay inside these ranges and needn't reach their ends.
All inputs are finite; a program needn't handle non-finite values.
Results may differ from the reference program's by a relative error of at most 0.0095.
Values may be sent and summed in bfloat16 or wider, within the bound.
A program may use at most 128 MiB of HBM per device.

```python
import math
import jax
import jax.numpy as jnp
from jax import lax

HEADS = 32
HD = 256
HID = 256
WINDOW = 2048
D = 8192
GROUP = 2048
TOKENS = 16384


def draw_pair(key):
    base = jax.random.fold_in(key, 4242)
    key_first, key_second = jax.random.split(base)
    query_vals = jnp.clip(jax.random.normal(key_first, (TOKENS, D), jnp.float32), -6.0, 6.0)
    key_vals = jnp.clip(jax.random.normal(key_second, (TOKENS, D), jnp.float32), -6.0, 6.0)
    return (query_vals, key_vals)


def draw_queries(key, part):
    return draw_pair(key)[0].astype(jnp.bfloat16)


def draw_keys(key, part):
    return draw_pair(key)[1].astype(jnp.bfloat16)


def shard_levels(stream_key, extent, pieces, smallest, largest):
    def one(dim, blocks):
        steps = jax.random.uniform(jax.random.fold_in(jax.random.fold_in(stream_key, 6), dim), (blocks,), jnp.float32, smallest / len(pieces), largest / len(pieces))
        return jnp.repeat(jnp.exp(steps), extent[dim] // blocks).reshape((-1,) + (1,) * (len(extent) - dim - 1))

    loudness = one(*pieces[0])
    for cut in pieces[1:]:
        loudness = loudness * one(*cut)
    return loudness


def scatter_about(key, extent, scale, bound, pieces=(), kind=jnp.bfloat16):
    level = shard_levels(key, extent, pieces, -0.22, 0.18) if pieces else 1.0
    array = jax.random.normal(key, extent, jnp.float32) * scale * level
    return jnp.minimum(jnp.maximum(array, -bound), bound).astype(kind)


def setup_inputs(seed: int = 0) -> dict:
    splits = jax.random.split(jax.random.key(seed), 7)
    return {
        "queries": draw_queries(jax.random.fold_in(splits[6], 71), 0),
        "keys": draw_keys(jax.random.fold_in(splits[6], 71), 0),
        "values": scatter_about(splits[2], (TOKENS, D), 1.0, 6.0, ((0, 128),)),
        "rates": jnp.clip(jnp.exp(math.log(0.0099487305) - 2.2979944 * jax.random.uniform(splits[3], (TOKENS, HEADS), jnp.float32) ** shard_levels(splits[3], (TOKENS, HEADS), ((0, 128),), -0.2, 0.2)), 0.0009994507, 0.0099487305).astype(jnp.bfloat16),
        "fast_init": scatter_about(splits[4], (3, HEADS, HID, HD), HD ** -0.5, 0.375, ((1, 16),)),
        "gain": jnp.clip(1.0 + 0.15 * jax.random.normal(splits[5], (D,), jnp.float32), 0.25, 1.75),
    }


EPSILON = 1e-06

def silu_parts(pre):
    sigma = jax.nn.sigmoid(pre)
    return (pre * sigma, sigma)

def attention_head(query_head, key_head, value_head):
    block = min(512, TOKENS)
    scale = HD ** (-0.5)
    key_pad = jnp.concatenate([jnp.zeros((WINDOW, HD), jnp.bfloat16), key_head], 0)
    value_pad = jnp.concatenate([jnp.zeros((WINDOW, HD), jnp.bfloat16), value_head], 0)

    def attend(number):
        start = number * block
        query_block = lax.dynamic_slice_in_dim(query_head, start, block, 0)
        key_block = lax.dynamic_slice_in_dim(key_pad, start, block + WINDOW, 0)
        value_block = lax.dynamic_slice_in_dim(value_pad, start, block + WINDOW, 0)
        scores = jnp.dot(query_block, key_block.T, preferred_element_type=jnp.float32) * scale
        query_pos = start + jnp.arange(block, dtype=jnp.int32)[:, None]
        key_pos = start - WINDOW + jnp.arange(block + WINDOW, dtype=jnp.int32)[None, :]
        valid = (key_pos <= query_pos) & (key_pos > query_pos - WINDOW) & (key_pos >= 0)
        masked = jnp.where(valid, scores, -jnp.inf)
        top = lax.optimization_barrier(jnp.max(masked, axis=1, keepdims=True))
        weights = jnp.where(valid, jnp.exp(masked - top), 0.0)
        probs = (weights / lax.optimization_barrier(jnp.sum(weights, axis=1, keepdims=True))).astype(jnp.bfloat16)
        return jnp.dot(probs, value_block, preferred_element_type=jnp.float32)
    parts = lax.map(attend, jnp.arange(TOKENS // block, dtype=jnp.int32))
    return parts.reshape(TOKENS, HD)

def group_update(group_keys, group_values, group_rates, weights):
    gate_pre = jnp.dot(group_keys, weights[0].T, preferred_element_type=jnp.float32)
    up_pre = jnp.dot(group_keys, weights[1].T, preferred_element_type=jnp.float32)
    gate_act, sigma = silu_parts(gate_pre)
    hidden = (gate_act * up_pre).astype(jnp.bfloat16)
    targets = (group_rates[:, None] * group_values.astype(jnp.float32)).astype(jnp.bfloat16)
    back = jnp.dot(targets, weights[2].T, preferred_element_type=jnp.float32)
    back_gate = (back * up_pre * sigma * (1.0 + gate_pre * (1.0 - sigma))).astype(jnp.bfloat16)
    back_up = (back * gate_act).astype(jnp.bfloat16)
    return jnp.stack([jnp.dot(back_gate.T, group_keys, preferred_element_type=jnp.float32), jnp.dot(back_up.T, group_keys, preferred_element_type=jnp.float32), jnp.dot(hidden.T, targets, preferred_element_type=jnp.float32)])

def apply_group(group_queries, prior, weights):
    initial = weights.astype(jnp.float32)
    target_ms = lax.optimization_barrier(jnp.mean(initial * initial, axis=-1, keepdims=True))
    renewed = initial + prior
    current = lax.optimization_barrier(jnp.mean(renewed * renewed, axis=-1, keepdims=True))
    fitted = (renewed * jnp.sqrt(target_ms) * lax.rsqrt(current + EPSILON)).astype(jnp.bfloat16)
    q_gate = jnp.dot(group_queries, fitted[0].T, preferred_element_type=jnp.float32)
    q_up = jnp.dot(group_queries, fitted[1].T, preferred_element_type=jnp.float32)
    q_hidden = (silu_parts(q_gate)[0] * q_up).astype(jnp.bfloat16)
    return jnp.dot(q_hidden, fitted[2], preferred_element_type=jnp.float32)

def reference(queries, keys, values, rates, fast_init, gain):
    count = TOKENS // GROUP

    def one_head(head):
        start = head * HD
        query_head = lax.dynamic_slice_in_dim(queries, start, HD, 1)
        key_head = lax.dynamic_slice_in_dim(keys, start, HD, 1)
        value_head = lax.dynamic_slice_in_dim(values, start, HD, 1)
        rate_head = lax.dynamic_slice_in_dim(rates, head, 1, 1)[:, 0].astype(jnp.float32)
        weights = lax.dynamic_index_in_dim(fast_init, head, 1, keepdims=False)
        attended = attention_head(query_head, key_head, value_head)
        updates = lax.map(lambda item: group_update(item[0], item[1], item[2], weights), (key_head.reshape(count, GROUP, HD), value_head.reshape(count, GROUP, HD), rate_head.reshape(count, GROUP)))
        running = jnp.cumsum(updates, axis=0)
        prior = jnp.concatenate([jnp.zeros((1,) + updates.shape[1:], jnp.float32), running[:-1]], 0)
        recalled = lax.map(lambda item: apply_group(item[0], item[1], weights), (query_head.reshape(count, GROUP, HD), prior))
        return attended + recalled.reshape(TOKENS, HD)
    combined = lax.map(one_head, jnp.arange(HEADS, dtype=jnp.int32))
    combined = jnp.transpose(combined, (1, 0, 2)).reshape(TOKENS, D)
    factor = lax.rsqrt(lax.optimization_barrier(jnp.mean(combined * combined, axis=1, keepdims=True)) + EPSILON)
    return (combined * factor * gain).astype(jnp.bfloat16)
```

```python
import functools

import jax
import jax.numpy as jnp
from jax import lax
from jax.experimental import pallas as pl
from jax.experimental.pallas import tpu as pltpu
from jax.sharding import PartitionSpec as P

F32 = jnp.float32
BF16 = jnp.bfloat16
MESH = pl.DeviceIdType.MESH
EPSILON = 1e-06
NT = (((1,), (1,)), ((), ()))
NN = (((1,), (0,)), ((), ()))
TN = (((0,), (0,)), ((), ()))

CTX = 8
PEERS = 16
GROUP = 2048
ROWS = 128
COLS = 512
HD = 256
BLOCK = 256
BLOCKS = GROUP // BLOCK
SLICE = 6 * HD // CTX
SCALE = HD**-0.5 * 1.4426950408889634
LOW = -1e30
SUM_STEP = 1
FIT_STEP = 3

OFFSETS = (
    (0, 1), (1, 0), (0, 3), (3, 0), (1, 1), (3, 3), (1, 3), (3, 1),
    (0, 2), (2, 0), (1, 2), (2, 1), (3, 2), (2, 3), (2, 2),
)


def dot(a, b, dims):
    return lax.dot_general(a, b, dims, preferred_element_type=F32)


def rows_of(index, size, base=0):
    return pl.ds(pl.multiple_of(base + index * size, size), size)


def head_columns(head):
    return slice(head * HD, head * HD + HD)


def attend(block, head, first, q_buf, k_buf, v_buf, s_buf, a_buf):
    cols = head_columns(head)
    here = rows_of(block, BLOCK)
    query = q_buf[here, cols]
    lane = lax.broadcasted_iota(jnp.int32, (BLOCK, HD), 1)
    row = lax.broadcasted_iota(jnp.int32, (BLOCK, HD), 0)
    far = lane > row

    def bias(tile):
        return jnp.where(jnp.logical_and(first, block + tile < BLOCKS), LOW, 0.0).astype(F32)

    def keys(tile):
        return k_buf[rows_of(block + tile, BLOCK), cols]

    def values(tile):
        return v_buf[rows_of(block + tile, BLOCK), cols]

    score = jnp.where(far, dot(query, keys(0), NT) + bias(0), dot(query, keys(BLOCKS), NT))
    s_buf[head, :, 0:HD] = score
    top = jnp.maximum(score[:, :128], score[:, 128:])
    for tile in range(1, BLOCKS):
        score = dot(query, keys(tile), NT)
        s_buf[head, :, tile * HD : tile * HD + HD] = score
        top = jnp.maximum(top, jnp.maximum(score[:, :128], score[:, 128:]) + bias(tile))
    top = jnp.max(top, axis=1, keepdims=True) * SCALE
    prob = jnp.exp2(s_buf[head, :, 0:HD] * SCALE - top)
    total = prob[:, :128] + prob[:, 128:]
    out = dot(jnp.where(far, prob, 0.0).astype(BF16), values(0), NN)
    out = out + dot(jnp.where(far, 0.0, prob).astype(BF16), values(BLOCKS), NN)
    for tile in range(1, BLOCKS):
        prob = jnp.exp2(s_buf[head, :, tile * HD : tile * HD + HD] * SCALE + (bias(tile) * SCALE - top))
        total = total + (prob[:, :128] + prob[:, 128:])
        out = out + dot(prob.astype(BF16), values(tile), NN)
    a_buf[here, cols] = out / jnp.sum(total, axis=1, keepdims=True)


def recall(block, head, q_buf, f_buf, a_buf, o_buf):
    cols = head_columns(head)
    here = rows_of(block, BLOCK)
    query = q_buf[here, cols]
    gate = dot(query, f_buf[head], NT)
    up = dot(query, f_buf[2 + head], NT)
    hidden = (gate * jax.nn.sigmoid(gate) * up).astype(BF16)
    o_buf[here, cols] = (a_buf[here, cols] + dot(hidden, f_buf[4 + head], NN)).astype(BF16)


def update(block, head, k_buf, v_buf, r_buf, w_ref, u_buf):
    cols = head_columns(head)
    here = rows_of(block, BLOCK, GROUP)
    key = k_buf[here, cols]
    value = v_buf[here, cols]
    rate = jnp.concatenate([r_buf[2 * block].T, r_buf[2 * block + 1].T], 0)[:, head : head + 1]
    target = (rate * value.astype(F32)).astype(BF16)
    gate = dot(key, w_ref[0, head], NT)
    up = dot(key, w_ref[1, head], NT)
    back = dot(target, w_ref[2, head], NT)
    sigma = jax.nn.sigmoid(gate)
    act = gate * sigma
    hidden = (act * up).astype(BF16)
    back_gate = (back * up * sigma * (1.0 + gate * (1.0 - sigma))).astype(BF16)
    back_up = (back * act).astype(BF16)
    for part, left, right in ((0, back_gate, key), (1, back_up, key), (2, hidden, target)):
        place = pl.ds((2 * part + head) * HD, HD)
        u_buf[place, :] += dot(left, right, TN)


def fit(part, w_ref, p_buf, f_buf):
    for head in range(2):
        initial = w_ref[part, head].astype(F32)
        renewed = initial + p_buf[pl.ds((2 * part + head) * HD, HD), :].astype(F32)
        wanted = jnp.mean(initial * initial, axis=1, keepdims=True)
        current = jnp.mean(renewed * renewed, axis=1, keepdims=True)
        f_buf[2 * part + head] = (renewed * jnp.sqrt(wanted) * lax.rsqrt(current + EPSILON)).astype(BF16)


def main_kernel(
    q_hbm, k_hbm, v_hbm, r_hbm, w_ref, out_hbm,
    q_buf, k_buf, v_buf, r_buf, s_buf, a_buf, o_buf, u_buf, ub_buf, u_in, p_out, p_buf, f_buf,
    q_in, k_in, v_in, r_in, o_in, q_sent, k_sent, v_sent, r_sent, o_sent,
    fk_in, fv_in, fk_sent, fv_sent, u_got, u_sent, p_got, p_sent,
):
    ctx = lax.axis_index("ctx")
    me = lax.axis_index("head")
    y, z = me // 4, me % 4
    first = ctx == 0
    after = (ctx + 1) % CTX
    peers = [((y + dy) % 4) * 4 + (z + dz) % 4 for dy, dz in OFFSETS]
    lines = [(ctx + step) % CTX for step in range(1, CTX)]

    barrier = pltpu.get_barrier_semaphore()
    for peer in peers:
        pl.semaphore_signal(barrier, inc=1, device_id=(ctx, peer), device_id_type=MESH)
    for line in lines:
        pl.semaphore_signal(barrier, inc=1, device_id=(line, me), device_id_type=MESH)
    pl.semaphore_wait(barrier, len(peers) + len(lines))

    def remote(src, dst, sent, got, where):
        return pltpu.make_async_remote_copy(
            src_ref=src, dst_ref=dst, send_sem=sent, recv_sem=got, device_id=where, device_id_type=MESH
        )

    def columns(ref, peer):
        return ref.at[:, pl.ds(pl.multiple_of(peer * COLS, COLS), COLS)]

    mine = rows_of(me, ROWS)
    mine_late = rows_of(me, ROWS, GROUP)

    def kv_sends(peer):
        return (
            remote(columns(k_hbm, peer), k_buf.at[mine_late], k_sent.at[peer], k_in.at[me], (ctx, peer)),
            remote(columns(v_hbm, peer), v_buf.at[mine_late], v_sent.at[peer], v_in.at[me], (ctx, peer)),
            remote(r_hbm.at[peer], r_buf.at[me], r_sent.at[peer], r_in.at[me], (ctx, peer)),
        )

    def q_send(peer):
        return remote(columns(q_hbm, peer), q_buf.at[mine], q_sent.at[peer], q_in.at[me], (ctx, peer))

    pltpu.make_async_copy(columns(k_hbm, me), k_buf.at[mine_late], k_in.at[me]).start()
    pltpu.make_async_copy(columns(v_hbm, me), v_buf.at[mine_late], v_in.at[me]).start()
    pltpu.make_async_copy(r_hbm.at[me], r_buf.at[me], r_in.at[me]).start()
    for peer in peers:
        for copy in kv_sends(peer):
            copy.start()
    pltpu.make_async_copy(columns(q_hbm, me), q_buf.at[mine], q_in.at[me]).start()
    for peer in peers:
        q_send(peer).start()

    def arrived(ref, sem):
        pltpu.make_async_copy(ref, ref, sem).wait()

    def block_at(step):
        turn = step // 2
        dy = turn + turn // 2 - 2 * (turn // 3)
        return ((y + 4 - dy) % 4) * 2 + (z // 2 + step) % 2

    def forwards(block):
        late, early = rows_of(block, BLOCK, GROUP), rows_of(block, BLOCK)
        return (
            remote(k_buf.at[late], k_buf.at[early], fk_sent.at[block], fk_in.at[block], (after, me)),
            remote(v_buf.at[late], v_buf.at[early], fv_sent.at[block], fv_in.at[block], (after, me)),
        )

    u_buf[...] = jnp.zeros_like(u_buf)

    @pl.loop(0, BLOCKS)
    def _(step):
        block = block_at(step)
        for half in range(2):
            source = 2 * block + half
            here = rows_of(source, ROWS, GROUP)
            arrived(k_buf.at[here], k_in.at[source])
            arrived(v_buf.at[here], v_in.at[source])
            arrived(r_buf.at[source], r_in.at[source])
        for copy in forwards(block):
            copy.start()
        for head in range(2):
            update(block, head, k_buf, v_buf, r_buf, w_ref, u_buf)

    def u_send(line):
        return remote(ub_buf.at[line], u_in.at[ctx], u_sent.at[line], u_got.at[ctx], (line, me))

    def p_send(line):
        return remote(p_out.at[line], p_buf.at[rows_of(ctx, SLICE)], p_sent.at[line], p_got.at[ctx], (line, me))

    for line in range(CTX):
        ub_buf[line] = u_buf[pl.ds(line * SLICE, SLICE), :].astype(BF16)
    for line in lines:
        u_send(line).start()
    u_in[ctx] = ub_buf[ctx]

    @pl.loop(0, BLOCKS)
    def _(block):
        early = rows_of(block, BLOCK)
        arrived(k_buf.at[early], fk_in.at[block])
        arrived(v_buf.at[early], fv_in.at[block])

    def o_send(source):
        here = rows_of(source, ROWS)
        return remote(
            o_buf.at[here], columns(out_hbm, me), o_sent.at[source], o_in.at[me], (ctx, source)
        )

    def o_local():
        return pltpu.make_async_copy(o_buf.at[mine], columns(out_hbm, me), o_in.at[me])

    def finish(block):
        for head in range(2):
            recall(block, head, q_buf, f_buf, a_buf, o_buf)
        for half in range(2):
            source = 2 * block + half

            @pl.when(source == me)
            def _():
                o_local().start()

            @pl.when(source != me)
            def _():
                o_send(source).start()

    @pl.loop(0, BLOCKS)
    def _(step):
        block = block_at(step)
        for half in range(2):
            source = 2 * block + half
            arrived(q_buf.at[rows_of(source, ROWS)], q_in.at[source])
        for head in range(2):
            attend(block, head, first, q_buf, k_buf, v_buf, s_buf, a_buf)

        @pl.when(step == SUM_STEP)
        def _():
            for line in lines:
                arrived(u_in.at[line], u_got.at[line])
            running = jnp.zeros((SLICE, HD), F32)
            for line in range(CTX):
                p_out[line] = running.astype(BF16)
                running = running + u_in[line].astype(F32)
            for line in lines:
                p_send(line).start()
            p_buf[rows_of(ctx, SLICE), :] = p_out[ctx]

        @pl.when(step == FIT_STEP)
        def _():
            for line in lines:
                arrived(p_buf.at[rows_of(line, SLICE)], p_got.at[line])
            for part in range(3):
                fit(part, w_ref, p_buf, f_buf)

            @pl.loop(0, FIT_STEP)
            def _(past):
                finish(block_at(past))

        @pl.when(step >= FIT_STEP)
        def _():
            finish(block)

    for peer in peers:
        for copy in kv_sends(peer):
            copy.wait_send()
        q_send(peer).wait_send()
    for line in lines:
        u_send(line).wait_send()
        p_send(line).wait_send()

    @pl.loop(0, BLOCKS)
    def _(block):
        for copy in forwards(block):
            copy.wait_send()

    for peer in peers:
        o_send(peer).wait_send()
        arrived(columns(out_hbm, peer), o_in.at[peer])
    arrived(columns(out_hbm, me), o_in.at[me])


def norm_kernel(x_ref, gain_ref, out_ref):
    wide = x_ref[...].astype(F32)
    factor = lax.rsqrt(jnp.mean(wide * wide, axis=1, keepdims=True) + EPSILON)
    out_ref[...] = (wide * factor * gain_ref[...]).astype(BF16)


def on_device(queries, keys, values, rates, fast_init, gain):
    rate_rows = jnp.pad(rates.astype(F32).T.reshape(PEERS, 2, ROWS), ((0, 0), (0, 6), (0, 0)))
    anywhere = pl.BlockSpec(memory_space=pl.ANY)
    near = pl.BlockSpec(memory_space=pltpu.VMEM)
    dma = pltpu.SemaphoreType.DMA
    wide = pl.pallas_call(
        main_kernel,
        out_shape=jax.ShapeDtypeStruct((ROWS, PEERS * COLS), BF16),
        in_specs=[anywhere, anywhere, anywhere, anywhere, near],
        out_specs=anywhere,
        scratch_shapes=[
            pltpu.VMEM((GROUP, COLS), BF16),
            pltpu.VMEM((2 * GROUP, COLS), BF16),
            pltpu.VMEM((2 * GROUP, COLS), BF16),
            pltpu.VMEM((PEERS, 8, ROWS), F32),
            pltpu.VMEM((2, BLOCK, GROUP), F32),
            pltpu.VMEM((GROUP, COLS), F32),
            pltpu.VMEM((GROUP, COLS), BF16),
            pltpu.VMEM((6 * HD, HD), F32),
            pltpu.VMEM((CTX, SLICE, HD), BF16),
            pltpu.VMEM((CTX, SLICE, HD), BF16),
            pltpu.VMEM((CTX, SLICE, HD), BF16),
            pltpu.VMEM((6 * HD, HD), BF16),
            pltpu.VMEM((6, HD, HD), BF16),
        ]
        + [dma((PEERS,))] * 10
        + [dma((BLOCKS,))] * 4
        + [dma((CTX,))] * 4,
        compiler_params=pltpu.CompilerParams(
            collective_id=0, has_side_effects=True, vmem_limit_bytes=48 * 2**20
        ),
        name="layer",
    )(queries, keys, values, rate_rows, fast_init)
    tile = 32
    return pl.pallas_call(
        norm_kernel,
        grid=(ROWS // tile,),
        out_shape=jax.ShapeDtypeStruct((ROWS, PEERS * COLS), BF16),
        in_specs=[
            pl.BlockSpec((tile, PEERS * COLS), lambda i: (i, 0)),
            pl.BlockSpec((1, PEERS * COLS), lambda i: (0, 0)),
        ],
        out_specs=pl.BlockSpec((tile, PEERS * COLS), lambda i: (i, 0)),
        name="norm",
    )(wide, gain.reshape(1, -1))


def solution(mesh):
    rows = P(("ctx", "head"), None)
    return jax.shard_map(
        on_device,
        mesh=mesh,
        in_specs=(rows, rows, rows, rows, P(None, "head", None, None), P()),
        out_specs=rows,
        check_vma=False,
    )
```

```python
import functools

import jax
import jax.numpy as jnp
from jax import lax
from jax.experimental import pallas as pl
from jax.experimental.pallas import tpu as pltpu
from jax.sharding import PartitionSpec as P

F32 = jnp.float32
BF16 = jnp.bfloat16
MESH = pl.DeviceIdType.MESH
EPSILON = 1e-06
NT = (((1,), (1,)), ((), ()))
NN = (((1,), (0,)), ((), ()))
TN = (((0,), (0,)), ((), ()))

CTX = 8
PEERS = 16
GROUP = 2048
ROWS = 128
COLS = 512
HD = 256
BLOCK = 256
BLOCKS = GROUP // BLOCK
SLICE = 6 * HD // CTX
SCALE = HD**-0.5 * 1.4426950408889634
LOW = -1e30
SUM_STEP = 1
FIT_STEP = 3

TURNS = (1, 3, 2)

OFFSETS = (
    (0, 1), (1, 0), (0, 3), (3, 0), (1, 1), (3, 3), (1, 3), (3, 1),
    (0, 2), (2, 0), (1, 2), (2, 1), (3, 2), (2, 3), (2, 2),
)
SLOTS = ((1, 1), (3, 1), (1, 3), (3, 3), (1, 2), (3, 2), (2, 1), (2, 3), (2, 2))


def dot(a, b, dims):
    return lax.dot_general(a, b, dims, preferred_element_type=F32)


def rows_of(index, size, base=0):
    return pl.ds(pl.multiple_of(base + index * size, size), size)


def head_columns(head):
    return slice(head * HD, head * HD + HD)


def attend(block, head, first, q_buf, k_buf, v_buf, s_buf, a_buf):
    cols = head_columns(head)
    here = rows_of(block, BLOCK)
    query = q_buf[here, cols]
    lane = lax.broadcasted_iota(jnp.int32, (BLOCK, HD), 1)
    row = lax.broadcasted_iota(jnp.int32, (BLOCK, HD), 0)
    far = lane > row

    def bias(tile):
        return jnp.where(jnp.logical_and(first, block + tile < BLOCKS), LOW, 0.0).astype(F32)

    def keys(tile):
        return k_buf[rows_of(block + tile, BLOCK), cols]

    def values(tile):
        return v_buf[rows_of(block + tile, BLOCK), cols]

    score = jnp.where(far, dot(query, keys(0), NT) + bias(0), dot(query, keys(BLOCKS), NT))
    s_buf[head, :, 0:HD] = score
    top = jnp.maximum(score[:, :128], score[:, 128:])
    for tile in range(1, BLOCKS):
        score = dot(query, keys(tile), NT)
        s_buf[head, :, tile * HD : tile * HD + HD] = score
        top = jnp.maximum(top, jnp.maximum(score[:, :128], score[:, 128:]) + bias(tile))
    top = jnp.max(top, axis=1, keepdims=True) * SCALE
    prob = jnp.exp2(s_buf[head, :, 0:HD] * SCALE - top)
    total = prob[:, :128] + prob[:, 128:]
    out = dot(jnp.where(far, prob, 0.0).astype(BF16), values(0), NN)
    out = out + dot(jnp.where(far, 0.0, prob).astype(BF16), values(BLOCKS), NN)
    for tile in range(1, BLOCKS):
        prob = jnp.exp2(s_buf[head, :, tile * HD : tile * HD + HD] * SCALE + (bias(tile) * SCALE - top))
        total = total + (prob[:, :128] + prob[:, 128:])
        out = out + dot(prob.astype(BF16), values(tile), NN)
    a_buf[here, cols] = out / jnp.sum(total, axis=1, keepdims=True)


def recall(block, head, q_buf, f_buf, a_buf, o_buf):
    cols = head_columns(head)
    here = rows_of(block, BLOCK)
    query = q_buf[here, cols]
    gate = dot(query, f_buf[head], NT)
    up = dot(query, f_buf[2 + head], NT)
    hidden = (gate * jax.nn.sigmoid(gate) * up).astype(BF16)
    o_buf[here, cols] = (a_buf[here, cols] + dot(hidden, f_buf[4 + head], NN)).astype(BF16)


def update(block, head, k_buf, v_buf, r_buf, w_ref, u_buf):
    cols = head_columns(head)
    here = rows_of(block, BLOCK, GROUP)
    key = k_buf[here, cols]
    value = v_buf[here, cols]
    rate = jnp.concatenate([r_buf[2 * block].T, r_buf[2 * block + 1].T], 0)[:, head : head + 1]
    target = (rate * value.astype(F32)).astype(BF16)
    gate = dot(key, w_ref[0, head], NT)
    up = dot(key, w_ref[1, head], NT)
    back = dot(target, w_ref[2, head], NT)
    sigma = jax.nn.sigmoid(gate)
    act = gate * sigma
    hidden = (act * up).astype(BF16)
    back_gate = (back * up * sigma * (1.0 + gate * (1.0 - sigma))).astype(BF16)
    back_up = (back * act).astype(BF16)
    for part, left, right in ((0, back_gate, key), (1, back_up, key), (2, hidden, target)):
        place = pl.ds((2 * part + head) * HD, HD)
        u_buf[place, :] += dot(left, right, TN)


def fit(part, w_ref, p_buf, f_buf):
    for head in range(2):
        initial = w_ref[part, head].astype(F32)
        renewed = initial + p_buf[pl.ds((2 * part + head) * HD, HD), :].astype(F32)
        wanted = jnp.mean(initial * initial, axis=1, keepdims=True)
        current = jnp.mean(renewed * renewed, axis=1, keepdims=True)
        f_buf[2 * part + head] = (renewed * jnp.sqrt(wanted) * lax.rsqrt(current + EPSILON)).astype(BF16)


def main_kernel(
    q_hbm, k_hbm, v_hbm, r_hbm, w_ref, out_hbm,
    q_buf, k_buf, v_buf, t_buf, r_buf, s_buf, a_buf, o_buf, u_buf, ub_buf, u_in, p_out, p_buf, f_buf,
    q_in, k_in, v_in, r_in, o_in, q_sent, k_sent, v_sent, r_sent, o_sent,
    fk_in, fv_in, fk_sent, fv_sent, t_in, tk_sent, tv_sent, ak_sent, av_sent, u_got, u_sent, p_got, p_sent,
):
    ctx = lax.axis_index("ctx")
    me = lax.axis_index("head")
    y, z = me // 4, me % 4
    first = ctx == 0
    after = (ctx + 1) % CTX
    peers = [((y + dy) % 4) * 4 + (z + dz) % 4 for dy, dz in OFFSETS]
    lines = [(ctx + step) % CTX for step in range(1, CTX)]

    barrier = pltpu.get_barrier_semaphore()
    for peer in peers:
        pl.semaphore_signal(barrier, inc=1, device_id=(ctx, peer), device_id_type=MESH)
    for line in lines:
        pl.semaphore_signal(barrier, inc=1, device_id=(line, me), device_id_type=MESH)
    pl.semaphore_wait(barrier, len(peers) + len(lines))

    def remote(src, dst, sent, got, where):
        return pltpu.make_async_remote_copy(
            src_ref=src, dst_ref=dst, send_sem=sent, recv_sem=got, device_id=where, device_id_type=MESH
        )

    def columns(ref, peer):
        return ref.at[:, pl.ds(pl.multiple_of(peer * COLS, COLS), COLS)]

    mine = rows_of(me, ROWS)
    mine_late = rows_of(me, ROWS, GROUP)

    def device_at(dy, dz):
        return ((y + dy + 4) % 4) * 4 + (z + dz + 4) % 4

    def kv_sends(peer):
        return (
            remote(columns(k_hbm, peer), k_buf.at[mine_late], k_sent.at[peer], k_in.at[me], (ctx, peer)),
            remote(columns(v_hbm, peer), v_buf.at[mine_late], v_sent.at[peer], v_in.at[me], (ctx, peer)),
        )

    def r_send(peer):
        return remote(r_hbm.at[peer], r_buf.at[me], r_sent.at[peer], r_in.at[me], (ctx, peer))

    def slot_sends(slot):
        dz, dy = SLOTS[slot]
        peer, way = device_at(dy, dz), device_at(0, dz)
        return (
            remote(columns(k_hbm, peer), t_buf.at[slot, 0], tk_sent.at[slot], t_in.at[slot], (ctx, way)),
            remote(columns(v_hbm, peer), t_buf.at[slot, 1], tv_sent.at[slot], t_in.at[slot], (ctx, way)),
        )

    def relays(slot):
        dz, dy = SLOTS[slot]
        source, peer = device_at(0, -dz), device_at(dy, 0)
        there = rows_of(source, ROWS, GROUP)
        return (
            remote(t_buf.at[slot, 0], k_buf.at[there], ak_sent.at[slot], k_in.at[source], (ctx, peer)),
            remote(t_buf.at[slot, 1], v_buf.at[there], av_sent.at[slot], v_in.at[source], (ctx, peer)),
        )

    def q_send(peer):
        return remote(columns(q_hbm, peer), q_buf.at[mine], q_sent.at[peer], q_in.at[me], (ctx, peer))

    pltpu.make_async_copy(columns(k_hbm, me), k_buf.at[mine_late], k_in.at[me]).start()
    pltpu.make_async_copy(columns(v_hbm, me), v_buf.at[mine_late], v_in.at[me]).start()
    pltpu.make_async_copy(r_hbm.at[me], r_buf.at[me], r_in.at[me]).start()
    for peer in peers:
        r_send(peer).start()
    straight = [device_at(dy, 0) for dy in TURNS] + [device_at(0, dz) for dz in TURNS]
    for peer in straight[:3]:
        for copy in kv_sends(peer):
            copy.start()
    for slot in range(6):
        for copy in slot_sends(slot):
            copy.start()
    for peer in straight[3:5]:
        for copy in kv_sends(peer):
            copy.start()
    for slot in range(6, len(SLOTS)):
        for copy in slot_sends(slot):
            copy.start()
    for copy in kv_sends(straight[5]):
        copy.start()

    def arrived(ref, sem):
        pltpu.make_async_copy(ref, ref, sem).wait()

    def turn_at(step):
        late = (step + 6) // 8
        far = step // 6
        spot = step % 2
        dy = late * ((1 + 2 * spot) * (1 - far) + 2 * far)
        other = (1 - late + far) * spot + (step // 4) * (1 - far)
        return dy, other

    def block_at(step):
        dy, other = turn_at(step)
        return ((y + 4 - dy) % 4) * 2 + (z // 2 + other) % 2

    q_peers = []
    for step in range(BLOCKS - 1):
        dy, other = turn_at(step)
        pair = ((y + dy) % 4) * 4 + 2 * ((z // 2 + other) % 2)
        q_peers += [pair, pair + 1]
    q_peers.append(y * 4 + z + 1 - 2 * (z % 2))

    def forwards(source):
        late, early = rows_of(source, ROWS, GROUP), rows_of(source, ROWS)
        return (
            remote(k_buf.at[late], k_buf.at[early], fk_sent.at[source], fk_in.at[source], (after, me)),
            remote(v_buf.at[late], v_buf.at[early], fv_sent.at[source], fv_in.at[source], (after, me)),
        )

    def forward(dy, dz):
        source = device_at(-dy, dz)
        late = rows_of(source, ROWS, GROUP)
        arrived(k_buf.at[late], k_in.at[source])
        arrived(v_buf.at[late], v_in.at[source])
        arrived(r_buf.at[source], r_in.at[source])
        for copy in forwards(source):
            copy.start()

    def relay(slot):
        arrived(t_buf.at[slot], t_in.at[slot])
        for copy in relays(slot):
            copy.start()

    def updates(dy, other):
        block = ((y + 4 - dy) % 4) * 2 + (z // 2 + other) % 2
        for head in range(2):
            update(block, head, k_buf, v_buf, r_buf, w_ref, u_buf)

    forward(0, 0)
    u_buf[...] = jnp.zeros_like(u_buf)
    relay(0)
    relay(1)
    forward(1, 0)
    forward(3, 0)
    relay(2)
    relay(3)
    forward(2, 0)
    relay(4)
    relay(5)
    forward(1, -1)
    forward(3, -1)
    forward(0, -1)
    forward(0, 1)
    updates(0, 0)
    forward(1, 1)
    forward(3, 1)
    updates(1, 0)
    relay(6)
    updates(3, 0)
    relay(7)
    forward(2, -1)
    relay(8)
    pltpu.make_async_copy(columns(q_hbm, me), q_buf.at[mine], q_in.at[me]).start()
    for peer in peers:
        q_send(peer).start()
    forward(2, 1)
    updates(2, 0)
    forward(1, 2)
    updates(1, 1)
    forward(3, 2)
    updates(3, 1)
    forward(2, 2)
    updates(2, 1)
    forward(0, 2)
    updates(0, 1)

    def u_send(line):
        return remote(ub_buf.at[line], u_in.at[ctx], u_sent.at[line], u_got.at[ctx], (line, me))

    def p_send(line):
        return remote(p_out.at[line], p_buf.at[rows_of(ctx, SLICE)], p_sent.at[line], p_got.at[ctx], (line, me))

    for line in range(CTX):
        ub_buf[line] = u_buf[pl.ds(line * SLICE, SLICE), :].astype(BF16)
    for line in lines:
        u_send(line).start()
    u_in[ctx] = ub_buf[ctx]

    @pl.loop(0, PEERS)
    def _(source):
        early = rows_of(source, ROWS)
        arrived(k_buf.at[early], fk_in.at[source])
        arrived(v_buf.at[early], fv_in.at[source])

    def o_send(source):
        here = rows_of(source, ROWS)
        return remote(
            o_buf.at[here], columns(out_hbm, me), o_sent.at[source], o_in.at[me], (ctx, source)
        )

    def o_local():
        return pltpu.make_async_copy(o_buf.at[mine], columns(out_hbm, me), o_in.at[me])

    def finish(block):
        for head in range(2):
            recall(block, head, q_buf, f_buf, a_buf, o_buf)
        for half in range(2):
            source = 2 * block + half

            @pl.when(source == me)
            def _():
                o_local().start()

            @pl.when(source != me)
            def _():
                o_send(source).start()

    @pl.loop(0, BLOCKS)
    def _(step):
        block = block_at(step)
        for half in range(2):
            source = 2 * block + half
            arrived(q_buf.at[rows_of(source, ROWS)], q_in.at[source])
        for head in range(2):
            attend(block, head, first, q_buf, k_buf, v_buf, s_buf, a_buf)

        @pl.when(step == SUM_STEP)
        def _():
            for line in lines:
                arrived(u_in.at[line], u_got.at[line])
            running = jnp.zeros((SLICE, HD), F32)
            for line in range(CTX):
                p_out[line] = running.astype(BF16)
                running = running + u_in[line].astype(F32)
            for line in lines:
                p_send(line).start()
            p_buf[rows_of(ctx, SLICE), :] = p_out[ctx]

        @pl.when(step == FIT_STEP)
        def _():
            for line in lines:
                arrived(p_buf.at[rows_of(line, SLICE)], p_got.at[line])
            for part in range(3):
                fit(part, w_ref, p_buf, f_buf)

            @pl.loop(0, FIT_STEP)
            def _(past):
                finish(block_at(past))

        @pl.when(step >= FIT_STEP)
        def _():
            finish(block)

    for peer in straight:
        for copy in kv_sends(peer):
            copy.wait_send()
    for slot in range(len(SLOTS)):
        for copy in slot_sends(slot) + relays(slot):
            copy.wait_send()
    for peer in peers:
        r_send(peer).wait_send()
        q_send(peer).wait_send()
    for line in lines:
        u_send(line).wait_send()
        p_send(line).wait_send()

    @pl.loop(0, PEERS)
    def _(source):
        for copy in forwards(source):
            copy.wait_send()

    for peer in peers:
        o_send(peer).wait_send()
        arrived(columns(out_hbm, peer), o_in.at[peer])
    arrived(columns(out_hbm, me), o_in.at[me])


def norm_kernel(x_ref, gain_ref, out_ref):
    wide = x_ref[...].astype(F32)
    factor = lax.rsqrt(jnp.mean(wide * wide, axis=1, keepdims=True) + EPSILON)
    out_ref[...] = (wide * factor * gain_ref[...]).astype(BF16)


def on_device(queries, keys, values, rates, fast_init, gain):
    rate_rows = jnp.pad(rates.astype(F32).T.reshape(PEERS, 2, ROWS), ((0, 0), (0, 6), (0, 0)))
    anywhere = pl.BlockSpec(memory_space=pl.ANY)
    near = pl.BlockSpec(memory_space=pltpu.VMEM)
    dma = pltpu.SemaphoreType.DMA
    wide = pl.pallas_call(
        main_kernel,
        out_shape=jax.ShapeDtypeStruct((ROWS, PEERS * COLS), BF16),
        in_specs=[anywhere, anywhere, anywhere, anywhere, near],
        out_specs=anywhere,
        scratch_shapes=[
            pltpu.VMEM((GROUP, COLS), BF16),
            pltpu.VMEM((2 * GROUP, COLS), BF16),
            pltpu.VMEM((2 * GROUP, COLS), BF16),
            pltpu.VMEM((len(SLOTS), 2, ROWS, COLS), BF16),
            pltpu.VMEM((PEERS, 8, ROWS), F32),
            pltpu.VMEM((2, BLOCK, GROUP), F32),
            pltpu.VMEM((GROUP, COLS), F32),
            pltpu.VMEM((GROUP, COLS), BF16),
            pltpu.VMEM((6 * HD, HD), F32),
            pltpu.VMEM((CTX, SLICE, HD), BF16),
            pltpu.VMEM((CTX, SLICE, HD), BF16),
            pltpu.VMEM((CTX, SLICE, HD), BF16),
            pltpu.VMEM((6 * HD, HD), BF16),
            pltpu.VMEM((6, HD, HD), BF16),
        ]
        + [dma((PEERS,))] * 10
        + [dma((PEERS,))] * 4
        + [dma((len(SLOTS),))] * 5
        + [dma((CTX,))] * 4,
        compiler_params=pltpu.CompilerParams(
            collective_id=0, has_side_effects=True, vmem_limit_bytes=60 * 2**20
        ),
        name="layer",
    )(queries, keys, values, rate_rows, fast_init)
    tile = 32
    return pl.pallas_call(
        norm_kernel,
        grid=(ROWS // tile,),
        out_shape=jax.ShapeDtypeStruct((ROWS, PEERS * COLS), BF16),
        in_specs=[
            pl.BlockSpec((tile, PEERS * COLS), lambda i: (i, 0)),
            pl.BlockSpec((1, PEERS * COLS), lambda i: (0, 0)),
        ],
        out_specs=pl.BlockSpec((tile, PEERS * COLS), lambda i: (i, 0)),
        name="norm",
    )(wide, gain.reshape(1, -1))


def solution(mesh):
    rows = P(("ctx", "head"), None)
    return jax.shard_map(
        on_device,
        mesh=mesh,
        in_specs=(rows, rows, rows, rows, P(None, "head", None, None), P()),
        out_specs=rows,
        check_vma=False,
    )
```

```python
import functools

import jax
import jax.numpy as jnp
from jax import lax
from jax.experimental import pallas as pl
from jax.experimental.pallas import tpu as pltpu
from jax.sharding import PartitionSpec as P

F32 = jnp.float32
BF16 = jnp.bfloat16
MESH = pl.DeviceIdType.MESH
EPSILON = 1e-06
NT = (((1,), (1,)), ((), ()))
NN = (((1,), (0,)), ((), ()))
TN = (((0,), (0,)), ((), ()))

CTX = 8
PEERS = 16
GROUP = 2048
ROWS = 128
COLS = 512
HD = 256
BLOCK = 256
BLOCKS = GROUP // BLOCK
SLICE = 6 * HD // CTX
SCALE = HD**-0.5 * 1.4426950408889634
LOW = -1e30
SUM_STEP = 1
FIT_STEP = 3

TURNS = (1, 3, 2)

OFFSETS = (
    (0, 1), (1, 0), (0, 3), (3, 0), (1, 1), (3, 3), (1, 3), (3, 1),
    (0, 2), (2, 0), (1, 2), (2, 1), (3, 2), (2, 3), (2, 2),
)
FAR = ((1, 1), (3, 3), (1, 3), (3, 1), (0, 2), (1, 2), (3, 2), (2, 0), (2, 1), (2, 3), (2, 2))
SLOTS = ((1, 1), (3, 1), (1, 3), (3, 3), (1, 2), (3, 2), (2, 1), (2, 3), (2, 2))


def dot(a, b, dims):
    return lax.dot_general(a, b, dims, preferred_element_type=F32)


def rows_of(index, size, base=0):
    return pl.ds(pl.multiple_of(base + index * size, size), size)


def head_columns(head):
    return slice(head * HD, head * HD + HD)


def attend(block, head, first, q_buf, k_buf, v_buf, s_buf, a_buf):
    cols = head_columns(head)
    here = rows_of(block, BLOCK)
    query = q_buf[here, cols]
    lane = lax.broadcasted_iota(jnp.int32, (BLOCK, HD), 1)
    row = lax.broadcasted_iota(jnp.int32, (BLOCK, HD), 0)
    far = lane > row

    def bias(tile):
        return jnp.where(jnp.logical_and(first, block + tile < BLOCKS), LOW, 0.0).astype(F32)

    def keys(tile):
        return k_buf[rows_of(block + tile, BLOCK), cols]

    def values(tile):
        return v_buf[rows_of(block + tile, BLOCK), cols]

    score = jnp.where(far, dot(query, keys(0), NT) + bias(0), dot(query, keys(BLOCKS), NT))
    s_buf[head, :, 0:HD] = score
    top = jnp.maximum(score[:, :128], score[:, 128:])
    for tile in range(1, BLOCKS):
        score = dot(query, keys(tile), NT)
        s_buf[head, :, tile * HD : tile * HD + HD] = score
        top = jnp.maximum(top, jnp.maximum(score[:, :128], score[:, 128:]) + bias(tile))
    top = jnp.max(top, axis=1, keepdims=True) * SCALE
    prob = jnp.exp2(s_buf[head, :, 0:HD] * SCALE - top)
    total = prob[:, :128] + prob[:, 128:]
    out = dot(jnp.where(far, prob, 0.0).astype(BF16), values(0), NN)
    out = out + dot(jnp.where(far, 0.0, prob).astype(BF16), values(BLOCKS), NN)
    for tile in range(1, BLOCKS):
        prob = jnp.exp2(s_buf[head, :, tile * HD : tile * HD + HD] * SCALE + (bias(tile) * SCALE - top))
        total = total + (prob[:, :128] + prob[:, 128:])
        out = out + dot(prob.astype(BF16), values(tile), NN)
    a_buf[here, cols] = out / jnp.sum(total, axis=1, keepdims=True)


def recall(block, head, q_buf, f_buf, a_buf, o_buf):
    cols = head_columns(head)
    here = rows_of(block, BLOCK)
    query = q_buf[here, cols]
    gate = dot(query, f_buf[head], NT)
    up = dot(query, f_buf[2 + head], NT)
    hidden = (gate * jax.nn.sigmoid(gate) * up).astype(BF16)
    o_buf[here, cols] = (a_buf[here, cols] + dot(hidden, f_buf[4 + head], NN)).astype(BF16)


def update(block, head, k_buf, v_buf, r_buf, w_ref, u_buf):
    cols = head_columns(head)
    here = rows_of(block, BLOCK, GROUP)
    key = k_buf[here, cols]
    value = v_buf[here, cols]
    rate = jnp.concatenate([r_buf[2 * block].T, r_buf[2 * block + 1].T], 0)[:, head : head + 1]
    target = (rate * value.astype(F32)).astype(BF16)
    gate = dot(key, w_ref[0, head], NT)
    up = dot(key, w_ref[1, head], NT)
    back = dot(target, w_ref[2, head], NT)
    sigma = jax.nn.sigmoid(gate)
    act = gate * sigma
    hidden = (act * up).astype(BF16)
    back_gate = (back * up * sigma * (1.0 + gate * (1.0 - sigma))).astype(BF16)
    back_up = (back * act).astype(BF16)
    for part, left, right in ((0, back_gate, key), (1, back_up, key), (2, hidden, target)):
        place = pl.ds((2 * part + head) * HD, HD)
        u_buf[place, :] += dot(left, right, TN)


def fit(part, w_ref, p_buf, f_buf):
    for head in range(2):
        initial = w_ref[part, head].astype(F32)
        renewed = initial + p_buf[pl.ds((2 * part + head) * HD, HD), :].astype(F32)
        wanted = jnp.mean(initial * initial, axis=1, keepdims=True)
        current = jnp.mean(renewed * renewed, axis=1, keepdims=True)
        f_buf[2 * part + head] = (renewed * jnp.sqrt(wanted) * lax.rsqrt(current + EPSILON)).astype(BF16)


def main_kernel(
    q_hbm, k_hbm, v_hbm, r_hbm, w_ref, out_hbm,
    q_buf, k_buf, v_buf, t_buf, rt_buf, r_buf, s_buf, a_buf, o_buf, o_in_slot, u_buf, ub_buf, u_in, p_out, p_buf, f_buf,
    q_in, k_in, v_in, o_in, q_sent, k_sent, v_sent, o_sent, rt_in, rt_sent, r_in, r_sent,
    fk_in, fv_in, fk_sent, fv_sent, t_in, tv_in, tk_sent, tv_sent, ak_sent, av_sent, ot_in, ot_sent, oa_sent, u_got, u_sent, p_got, p_sent,
):
    ctx = lax.axis_index("ctx")
    me = lax.axis_index("head")
    y, z = me // 4, me % 4
    first = ctx == 0
    after = (ctx + 1) % CTX
    peers = [((y + dy) % 4) * 4 + (z + dz) % 4 for dy, dz in OFFSETS]
    lines = [(ctx + step) % CTX for step in range(1, CTX)]

    barrier = pltpu.get_barrier_semaphore()
    for peer in peers:
        pl.semaphore_signal(barrier, inc=1, device_id=(ctx, peer), device_id_type=MESH)
    for line in lines:
        pl.semaphore_signal(barrier, inc=1, device_id=(line, me), device_id_type=MESH)
    pl.semaphore_wait(barrier, len(peers) + len(lines))

    def remote(src, dst, sent, got, where):
        return pltpu.make_async_remote_copy(
            src_ref=src, dst_ref=dst, send_sem=sent, recv_sem=got, device_id=where, device_id_type=MESH
        )

    def columns(ref, peer):
        return ref.at[:, pl.ds(pl.multiple_of(peer * COLS, COLS), COLS)]

    mine = rows_of(me, ROWS)
    mine_late = rows_of(me, ROWS, GROUP)

    def device_at(dy, dz):
        return ((y + dy + 4) % 4) * 4 + (z + dz + 4) % 4

    def kv_sends(peer):
        return (
            remote(columns(k_hbm, peer), k_buf.at[mine_late], k_sent.at[peer], k_in.at[me], (ctx, peer)),
            remote(columns(v_hbm, peer), v_buf.at[mine_late], v_sent.at[peer], v_in.at[me], (ctx, peer)),
        )

    def r_aside(dz):
        way = (z + dz) % 4
        return remote(r_hbm.at[:, way], rt_buf.at[z], rt_sent.at[dz], rt_in.at[z], (ctx, y * 4 + way))

    def r_relay(dy):
        way = (y + dy) % 4
        return remote(rt_buf.at[:, way], r_buf.at[rows_of(y, 4)], r_sent.at[dy], r_in.at[y], (ctx, way * 4 + z))

    def slot_sends(slot):
        dz, dy = SLOTS[slot]
        peer, way = device_at(dy, dz), device_at(0, dz)
        return (
            remote(columns(k_hbm, peer), t_buf.at[slot, 0], tk_sent.at[slot], t_in.at[slot], (ctx, way)),
            remote(columns(v_hbm, peer), t_buf.at[slot, 1], tv_sent.at[slot], tv_in.at[slot], (ctx, way)),
        )

    def relays(slot):
        dz, dy = SLOTS[slot]
        source, peer = device_at(0, -dz), device_at(dy, 0)
        there = rows_of(source, ROWS, GROUP)
        return (
            remote(t_buf.at[slot, 0], k_buf.at[there], ak_sent.at[slot], k_in.at[source], (ctx, peer)),
            remote(t_buf.at[slot, 1], v_buf.at[there], av_sent.at[slot], v_in.at[source], (ctx, peer)),
        )

    def q_send(peer):
        return remote(columns(q_hbm, peer), q_buf.at[mine], q_sent.at[peer], q_in.at[me], (ctx, peer))

    pltpu.make_async_copy(columns(k_hbm, me), k_buf.at[mine_late], k_in.at[me]).start()
    pltpu.make_async_copy(columns(v_hbm, me), v_buf.at[mine_late], v_in.at[me]).start()
    pltpu.make_async_copy(r_hbm.at[:, z], rt_buf.at[z], rt_in.at[z]).start()
    for dz in TURNS:
        r_aside(dz).start()
    straight = [device_at(dy, 0) for dy in TURNS] + [device_at(0, dz) for dz in TURNS]
    for peer in straight[:3]:
        for copy in kv_sends(peer):
            copy.start()
    for slot in range(6):
        for copy in slot_sends(slot):
            copy.start()
    for peer in straight[3:5]:
        for copy in kv_sends(peer):
            copy.start()

    def arrived(ref, sem):
        pltpu.make_async_copy(ref, ref, sem).wait()

    def turn_at(step):
        last = step // 6
        far = step // 4 - last
        near = 1 - far - last
        dy = near * (1 + 2 * (step % 2)) + 2 * far
        return dy, near * (step // 2) + far * (step % 2) + last * (1 - step % 2)

    def block_at(step):
        dy, other = turn_at(step)
        return ((y + 4 - dy) % 4) * 2 + (z // 2 + other) % 2

    near_peers = [device_at(*turn) for turn in ((1, 0), (3, 0), (0, 1), (0, 3))]
    far_peers = [device_at(*turn) for turn in FAR]

    def forwards(source):
        late, early = rows_of(source, ROWS, GROUP), rows_of(source, ROWS)
        return (
            remote(k_buf.at[late], k_buf.at[early], fk_sent.at[source], fk_in.at[source], (after, me)),
            remote(v_buf.at[late], v_buf.at[early], fv_sent.at[source], fv_in.at[source], (after, me)),
        )

    def forward(dy, dz):
        source = device_at(-dy, dz)
        late = rows_of(source, ROWS, GROUP)
        arrived(k_buf.at[late], k_in.at[source])
        arrived(v_buf.at[late], v_in.at[source])
        for copy in forwards(source):
            copy.start()

    def relay(slot, *more):
        for part, sem in ((0, t_in), (1, tv_in)):
            for each in (slot,) + more:
                arrived(t_buf.at[each, part], sem.at[each])
                relays(each)[part].start()

    def rates(dy):
        source = (y + 4 - dy) % 4
        arrived(r_buf.at[rows_of(source, 4)], r_in.at[source])

    def updates(dy, other):
        block = ((y + 4 - dy) % 4) * 2 + (z // 2 + other) % 2
        for head in range(2):
            update(block, head, k_buf, v_buf, r_buf, w_ref, u_buf)

    forward(0, 0)
    u_buf[...] = jnp.zeros_like(u_buf)
    for source in range(4):
        arrived(rt_buf.at[source], rt_in.at[source])
    for dy in TURNS:
        r_relay(dy).start()
    pltpu.make_async_copy(rt_buf.at[:, y], r_buf.at[rows_of(y, 4)], r_in.at[y]).start()
    relay(0, 1)
    forward(1, 0)
    forward(3, 0)
    relay(2, 3)
    forward(2, 0)
    relay(4, 5)
    forward(1, -1)
    forward(3, -1)
    forward(1, 1)
    forward(3, 1)
    forward(0, -1)
    forward(0, 1)
    for slot in range(6, len(SLOTS)):
        for copy in slot_sends(slot):
            copy.start()
    for copy in kv_sends(straight[5]):
        copy.start()
    for dy in range(4):
        rates(dy)
    updates(0, 0)
    updates(1, 0)
    relay(6)
    updates(3, 0)
    forward(2, -1)
    forward(2, 1)
    relay(7)
    updates(2, 0)
    relay(8)
    pltpu.make_async_copy(columns(q_hbm, me), q_buf.at[mine], q_in.at[me]).start()
    for peer in near_peers:
        q_send(peer).start()
    forward(1, 2)
    updates(1, 1)
    forward(3, 2)
    updates(3, 1)
    forward(0, 2)
    updates(0, 1)
    forward(2, 2)
    for peer in far_peers:
        q_send(peer).start()
    updates(2, 1)

    def u_send(line):
        return remote(ub_buf.at[line], u_in.at[ctx], u_sent.at[line], u_got.at[ctx], (line, me))

    def p_send(line):
        return remote(p_out.at[line], p_buf.at[rows_of(ctx, SLICE)], p_sent.at[line], p_got.at[ctx], (line, me))

    for line in range(CTX):
        ub_buf[line] = u_buf[pl.ds(line * SLICE, SLICE), :].astype(BF16)
    for line in lines:
        u_send(line).start()
    u_in[ctx] = ub_buf[ctx]

    @pl.loop(0, PEERS)
    def _(source):
        early = rows_of(source, ROWS)
        arrived(k_buf.at[early], fk_in.at[source])
        arrived(v_buf.at[early], fv_in.at[source])

    def o_send(source):
        here = rows_of(source, ROWS)
        return remote(
            o_buf.at[here], columns(out_hbm, me), o_sent.at[source], o_in.at[me], (ctx, source)
        )

    def o_local():
        return pltpu.make_async_copy(o_buf.at[mine], columns(out_hbm, me), o_in.at[me])

    def o_slot(dy, dz):
        return (dz - 1) * 3 + dy - 1

    def o_aside(source, slot):
        there = o_in_slot.at[slot]
        here = rows_of(source, ROWS)
        return remote(o_buf.at[here], there, ot_sent.at[slot], ot_in.at[slot], (ctx, y * 4 + source % 4))

    def o_relay(dy, from_z, slot):
        there = columns(out_hbm, y * 4 + from_z)
        peer = ((y + dy) % 4) * 4 + z
        return remote(o_in_slot.at[slot], there, oa_sent.at[slot], o_in.at[y * 4 + from_z], (ctx, peer))

    def finish(step):
        back, _ = turn_at(step)
        dy = (4 - back) % 4
        block = block_at(step)
        for head in range(2):
            recall(block, head, q_buf, f_buf, a_buf, o_buf)
        for half in range(2):
            source = 2 * block + half
            dz = (source + 4 - z) % 4

            @pl.when(source == me)
            def _():
                o_local().start()

            @pl.when(jnp.logical_and(source != me, dy * dz == 0))
            def _():
                o_send(source).start()

            @pl.when(dy * dz != 0)
            def _():
                o_aside(source, o_slot(dy, dz)).start()

    def pass_on(step):
        back, other = turn_at(step)
        dy = (4 - back) % 4
        for half in range(2):
            from_z = 2 * ((z // 2 + other) % 2) + half
            dz = (z + 4 - from_z) % 4

            @pl.when(dy * dz != 0)
            def _():
                slot = o_slot(dy, dz)
                arrived(o_in_slot.at[slot], ot_in.at[slot])
                o_relay(dy, from_z, slot).start()

    @pl.loop(0, BLOCKS)
    def _(step):
        block = block_at(step)
        for half in range(2):
            source = 2 * block + half
            arrived(q_buf.at[rows_of(source, ROWS)], q_in.at[source])
        for head in range(2):
            attend(block, head, first, q_buf, k_buf, v_buf, s_buf, a_buf)

        @pl.when(step == SUM_STEP)
        def _():
            for line in lines:
                arrived(u_in.at[line], u_got.at[line])
            running = jnp.zeros((SLICE, HD), F32)
            for line in range(CTX):
                p_out[line] = running.astype(BF16)
                running = running + u_in[line].astype(F32)
            for line in lines:
                p_send(line).start()
            p_buf[rows_of(ctx, SLICE), :] = p_out[ctx]

        @pl.when(step == FIT_STEP)
        def _():
            for line in lines:
                arrived(p_buf.at[rows_of(line, SLICE)], p_got.at[line])
            for part in range(3):
                fit(part, w_ref, p_buf, f_buf)

            @pl.loop(0, FIT_STEP)
            def _(past):
                finish(past)

        @pl.when(step >= FIT_STEP)
        def _():
            finish(step)

        @pl.when(step > FIT_STEP)
        def _():
            pass_on(step - FIT_STEP - 1)

    @pl.loop(BLOCKS - FIT_STEP - 1, BLOCKS - 2)
    def _(step):
        pass_on(step)

    for turn in TURNS:
        r_aside(turn).wait_send()
        r_relay(turn).wait_send()
    for peer in straight:
        for copy in kv_sends(peer):
            copy.wait_send()
    for slot in range(len(SLOTS)):
        for copy in slot_sends(slot) + relays(slot):
            copy.wait_send()
    for peer in peers:
        q_send(peer).wait_send()
    for line in lines:
        u_send(line).wait_send()
        p_send(line).wait_send()

    @pl.loop(0, PEERS)
    def _(source):
        for copy in forwards(source):
            copy.wait_send()

    for peer in straight:
        o_send(peer).wait_send()
    for dy, dz in OFFSETS:
        if dy * dz:
            slot = o_slot(dy, dz)
            o_aside(device_at(dy, dz), slot).wait_send()
            o_relay(dy, (z + 4 - dz) % 4, slot).wait_send()
    for peer in peers:
        arrived(columns(out_hbm, peer), o_in.at[peer])
    arrived(columns(out_hbm, me), o_in.at[me])


def norm_kernel(x_ref, gain_ref, out_ref):
    wide = x_ref[...].astype(F32)
    factor = lax.rsqrt(jnp.mean(wide * wide, axis=1, keepdims=True) + EPSILON)
    out_ref[...] = (wide * factor * gain_ref[...]).astype(BF16)


def on_device(queries, keys, values, rates, fast_init, gain):
    rate_rows = jnp.pad(rates.astype(F32).T.reshape(4, 4, 2, ROWS), ((0, 0), (0, 0), (0, 6), (0, 0)))
    anywhere = pl.BlockSpec(memory_space=pl.ANY)
    near = pl.BlockSpec(memory_space=pltpu.VMEM)
    dma = pltpu.SemaphoreType.DMA
    wide = pl.pallas_call(
        main_kernel,
        out_shape=jax.ShapeDtypeStruct((ROWS, PEERS * COLS), BF16),
        in_specs=[anywhere, anywhere, anywhere, anywhere, near],
        out_specs=anywhere,
        scratch_shapes=[
            pltpu.VMEM((GROUP, COLS), BF16),
            pltpu.VMEM((2 * GROUP, COLS), BF16),
            pltpu.VMEM((2 * GROUP, COLS), BF16),
            pltpu.VMEM((len(SLOTS), 2, ROWS, COLS), BF16),
            pltpu.VMEM((4, 4, 8, ROWS), F32),
            pltpu.VMEM((PEERS, 8, ROWS), F32),
            pltpu.VMEM((2, BLOCK, GROUP), F32),
            pltpu.VMEM((GROUP, COLS), F32),
            pltpu.VMEM((GROUP, COLS), BF16),
            pltpu.VMEM((len(SLOTS), ROWS, COLS), BF16),
            pltpu.VMEM((6 * HD, HD), F32),
            pltpu.VMEM((CTX, SLICE, HD), BF16),
            pltpu.VMEM((CTX, SLICE, HD), BF16),
            pltpu.VMEM((CTX, SLICE, HD), BF16),
            pltpu.VMEM((6 * HD, HD), BF16),
            pltpu.VMEM((6, HD, HD), BF16),
        ]
        + [dma((PEERS,))] * 8
        + [dma((4,))] * 4
        + [dma((PEERS,))] * 4
        + [dma((len(SLOTS),))] * 9
        + [dma((CTX,))] * 4,
        compiler_params=pltpu.CompilerParams(
            collective_id=0, has_side_effects=True, vmem_limit_bytes=60 * 2**20
        ),
        name="layer",
    )(queries, keys, values, rate_rows, fast_init)
    tile = 64
    return pl.pallas_call(
        norm_kernel,
        grid=(ROWS // tile,),
        out_shape=jax.ShapeDtypeStruct((ROWS, PEERS * COLS), BF16),
        in_specs=[
            pl.BlockSpec((tile, PEERS * COLS), lambda i: (i, 0)),
            pl.BlockSpec((1, PEERS * COLS), lambda i: (0, 0)),
        ],
        out_specs=pl.BlockSpec((tile, PEERS * COLS), lambda i: (i, 0)),
        name="norm",
    )(wide, gain.reshape(1, -1))


def solution(mesh):
    rows = P(("ctx", "head"), None)
    return jax.shard_map(
        on_device,
        mesh=mesh,
        in_specs=(rows, rows, rows, rows, P(None, "head", None, None), P()),
        out_specs=rows,
        check_vma=False,
    )
```

```python
import functools

import jax
import jax.numpy as jnp
from jax import lax
from jax.experimental import pallas as pl
from jax.experimental.pallas import tpu as pltpu
from jax.sharding import PartitionSpec as P

F32 = jnp.float32
BF16 = jnp.bfloat16
MESH = pl.DeviceIdType.MESH
EPSILON = 1e-06
NT = (((1,), (1,)), ((), ()))
NN = (((1,), (0,)), ((), ()))
TN = (((0,), (0,)), ((), ()))

CTX = 8
PEERS = 16
GROUP = 2048
ROWS = 128
COLS = 512
HD = 256
BLOCK = 256
BLOCKS = GROUP // BLOCK
SLICE = 6 * HD // CTX
SCALE = HD**-0.5 * 1.4426950408889634
LOW = -1e30
SUM_STEP = 0
FIT_STEP = 2

TURNS = (1, 3, 2)

OFFSETS = (
    (0, 1), (1, 0), (0, 3), (3, 0), (1, 1), (3, 3), (1, 3), (3, 1),
    (0, 2), (2, 0), (1, 2), (2, 1), (3, 2), (2, 3), (2, 2),
)
FAR = ((1, 1), (3, 3), (1, 3), (3, 1), (0, 2), (1, 2), (3, 2), (2, 0), (2, 1), (2, 3), (2, 2))
SLOTS = ((1, 1), (3, 1), (1, 3), (3, 3), (1, 2), (3, 2), (2, 1), (2, 3), (2, 2))


def dot(a, b, dims):
    return lax.dot_general(a, b, dims, preferred_element_type=F32)


def rows_of(index, size, base=0):
    return pl.ds(pl.multiple_of(base + index * size, size), size)


def head_columns(head):
    return slice(head * HD, head * HD + HD)


def attend(block, head, first, q_buf, k_buf, v_buf, s_buf, a_buf):
    cols = head_columns(head)
    here = rows_of(block, BLOCK)
    query = q_buf[here, cols]
    lane = lax.broadcasted_iota(jnp.int32, (BLOCK, HD), 1)
    row = lax.broadcasted_iota(jnp.int32, (BLOCK, HD), 0)
    far = lane > row

    def bias(tile):
        return jnp.where(jnp.logical_and(first, block + tile < BLOCKS), LOW, 0.0).astype(F32)

    def keys(tile):
        return k_buf[rows_of(block + tile, BLOCK), cols]

    def values(tile):
        return v_buf[rows_of(block + tile, BLOCK), cols]

    score = jnp.where(far, dot(query, keys(0), NT) + bias(0), dot(query, keys(BLOCKS), NT))
    s_buf[head, :, 0:HD] = score
    top = jnp.maximum(score[:, :128], score[:, 128:])
    for tile in range(1, BLOCKS):
        score = dot(query, keys(tile), NT)
        s_buf[head, :, tile * HD : tile * HD + HD] = score
        top = jnp.maximum(top, jnp.maximum(score[:, :128], score[:, 128:]) + bias(tile))
    top = jnp.max(top, axis=1, keepdims=True) * SCALE
    prob = jnp.exp2(s_buf[head, :, 0:HD] * SCALE - top)
    total = prob[:, :128] + prob[:, 128:]
    out = dot(jnp.where(far, prob, 0.0).astype(BF16), values(0), NN)
    out = out + dot(jnp.where(far, 0.0, prob).astype(BF16), values(BLOCKS), NN)
    for tile in range(1, BLOCKS):
        prob = jnp.exp2(s_buf[head, :, tile * HD : tile * HD + HD] * SCALE + (bias(tile) * SCALE - top))
        total = total + (prob[:, :128] + prob[:, 128:])
        out = out + dot(prob.astype(BF16), values(tile), NN)
    a_buf[here, cols] = out / jnp.sum(total, axis=1, keepdims=True)


def recall(block, head, q_buf, f_buf, a_buf, o_buf):
    cols = head_columns(head)
    here = rows_of(block, BLOCK)
    query = q_buf[here, cols]
    gate = dot(query, f_buf[head], NT)
    up = dot(query, f_buf[2 + head], NT)
    hidden = (gate * jax.nn.sigmoid(gate) * up).astype(BF16)
    o_buf[here, cols] = (a_buf[here, cols] + dot(hidden, f_buf[4 + head], NN)).astype(BF16)


def update(block, head, k_buf, v_buf, r_buf, w_ref, u_buf):
    cols = head_columns(head)
    here = rows_of(block, BLOCK, GROUP)
    key = k_buf[here, cols]
    value = v_buf[here, cols]
    lines = [r_buf[2 * block + half].astype(F32)[head : head + 1] for half in range(2)]
    rate = jnp.concatenate([jnp.broadcast_to(line, (8, ROWS)).T for line in lines], 0)[:, :1]
    target = (rate * value.astype(F32)).astype(BF16)
    gate = dot(key, w_ref[0, head], NT)
    up = dot(key, w_ref[1, head], NT)
    back = dot(target, w_ref[2, head], NT)
    sigma = jax.nn.sigmoid(gate)
    act = gate * sigma
    hidden = (act * up).astype(BF16)
    back_gate = (back * up * sigma * (1.0 + gate * (1.0 - sigma))).astype(BF16)
    back_up = (back * act).astype(BF16)
    for part, left, right in ((0, back_gate, key), (1, back_up, key), (2, hidden, target)):
        place = pl.ds((2 * part + head) * HD, HD)
        u_buf[place, :] += dot(left, right, TN)


def fit(part, w_ref, p_buf, f_buf):
    for head in range(2):
        initial = w_ref[part, head].astype(F32)
        renewed = initial + p_buf[pl.ds((2 * part + head) * HD, HD), :].astype(F32)
        wanted = jnp.mean(initial * initial, axis=1, keepdims=True)
        current = jnp.mean(renewed * renewed, axis=1, keepdims=True)
        f_buf[2 * part + head] = (renewed * jnp.sqrt(wanted) * lax.rsqrt(current + EPSILON)).astype(BF16)


def main_kernel(
    q_hbm, k_hbm, v_hbm, r_hbm, w_hbm, out_hbm,
    w_ref, w_in,
    q_buf, k_buf, v_buf, t_buf, rt_buf, r_buf, s_buf, a_buf, o_buf, o_in_slot, u_buf, ub_buf, u_in, p_out, p_buf, f_buf,
    q_in, k_in, v_in, o_in, q_sent, k_sent, v_sent, o_sent, rt_in, rt_sent, r_in, r_sent,
    fk_in, fv_in, fk_sent, fv_sent, t_in, tv_in, tk_sent, tv_sent, ak_sent, av_sent, ot_in, ot_sent, oa_sent, u_got, u_sent, p_got, p_sent,
):
    ctx = lax.axis_index("ctx")
    me = lax.axis_index("head")
    y, z = me // 4, me % 4
    first = ctx == 0
    after = (ctx + 1) % CTX
    peers = [((y + dy) % 4) * 4 + (z + dz) % 4 for dy, dz in OFFSETS]
    lines = [(ctx + step) % CTX for step in range(1, CTX)]

    barrier = pltpu.get_barrier_semaphore()
    for peer in peers:
        pl.semaphore_signal(barrier, inc=1, device_id=(ctx, peer), device_id_type=MESH)
    for line in lines:
        pl.semaphore_signal(barrier, inc=1, device_id=(line, me), device_id_type=MESH)
    weights = pltpu.make_async_copy(w_hbm, w_ref, w_in)
    weights.start()
    pl.semaphore_wait(barrier, len(peers) + len(lines))

    def remote(src, dst, sent, got, where):
        return pltpu.make_async_remote_copy(
            src_ref=src, dst_ref=dst, send_sem=sent, recv_sem=got, device_id=where, device_id_type=MESH
        )

    def columns(ref, peer):
        return ref.at[:, pl.ds(pl.multiple_of(peer * COLS, COLS), COLS)]

    mine = rows_of(me, ROWS)
    mine_late = rows_of(me, ROWS, GROUP)

    def device_at(dy, dz):
        return ((y + dy + 4) % 4) * 4 + (z + dz + 4) % 4

    def kv_sends(peer):
        return (
            remote(columns(k_hbm, peer), k_buf.at[mine_late], k_sent.at[peer], k_in.at[me], (ctx, peer)),
            remote(columns(v_hbm, peer), v_buf.at[mine_late], v_sent.at[peer], v_in.at[me], (ctx, peer)),
        )

    def r_aside(dz):
        way = (z + dz) % 4
        return remote(r_hbm.at[:, way], rt_buf.at[z], rt_sent.at[dz], rt_in.at[z], (ctx, y * 4 + way))

    def r_relay(dy):
        way = (y + dy) % 4
        return remote(rt_buf.at[:, way], r_buf.at[rows_of(y, 4)], r_sent.at[dy], r_in.at[y], (ctx, way * 4 + z))

    def slot_sends(slot):
        dz, dy = SLOTS[slot]
        peer, way = device_at(dy, dz), device_at(0, dz)
        return (
            remote(columns(k_hbm, peer), t_buf.at[slot, 0], tk_sent.at[slot], t_in.at[slot], (ctx, way)),
            remote(columns(v_hbm, peer), t_buf.at[slot, 1], tv_sent.at[slot], tv_in.at[slot], (ctx, way)),
        )

    def relays(slot):
        dz, dy = SLOTS[slot]
        source, peer = device_at(0, -dz), device_at(dy, 0)
        there = rows_of(source, ROWS, GROUP)
        return (
            remote(t_buf.at[slot, 0], k_buf.at[there], ak_sent.at[slot], k_in.at[source], (ctx, peer)),
            remote(t_buf.at[slot, 1], v_buf.at[there], av_sent.at[slot], v_in.at[source], (ctx, peer)),
        )

    def q_send(peer):
        return remote(columns(q_hbm, peer), q_buf.at[mine], q_sent.at[peer], q_in.at[me], (ctx, peer))

    pltpu.make_async_copy(columns(k_hbm, me), k_buf.at[mine_late], k_in.at[me]).start()
    pltpu.make_async_copy(columns(v_hbm, me), v_buf.at[mine_late], v_in.at[me]).start()
    pltpu.make_async_copy(r_hbm.at[:, z], rt_buf.at[z], rt_in.at[z]).start()
    for dz in TURNS:
        r_aside(dz).start()
    straight = [device_at(dy, 0) for dy in TURNS] + [device_at(0, dz) for dz in TURNS]
    for peer in straight[:3]:
        for copy in kv_sends(peer):
            copy.start()
    for slot in range(6):
        for copy in slot_sends(slot):
            copy.start()
    for peer in straight[3:5]:
        for copy in kv_sends(peer):
            copy.start()

    def arrived(ref, sem):
        pltpu.make_async_copy(ref, ref, sem).wait()

    def turn_at(step):
        last = step // 6
        far = step // 4 - last
        near = 1 - far - last
        dy = near * (1 + 2 * (step % 2)) + 2 * far
        return dy, near * (step // 2) + far * (step % 2) + last * (1 - step % 2)

    def block_at(step):
        dy, other = turn_at(step)
        return ((y + 4 - dy) % 4) * 2 + (z // 2 + other) % 2

    near_peers = [device_at(*turn) for turn in ((1, 0), (3, 0), (0, 1), (0, 3))]
    far_peers = [device_at(*turn) for turn in FAR]

    def forwards(source):
        late, early = rows_of(source, ROWS, GROUP), rows_of(source, ROWS)
        return (
            remote(k_buf.at[late], k_buf.at[early], fk_sent.at[source], fk_in.at[source], (after, me)),
            remote(v_buf.at[late], v_buf.at[early], fv_sent.at[source], fv_in.at[source], (after, me)),
        )

    def forward(dy, dz):
        source = device_at(-dy, dz)
        late = rows_of(source, ROWS, GROUP)
        arrived(k_buf.at[late], k_in.at[source])
        arrived(v_buf.at[late], v_in.at[source])
        for copy in forwards(source):
            copy.start()

    def relay(slot, *more):
        for part, sem in ((0, t_in), (1, tv_in)):
            for each in (slot,) + more:
                arrived(t_buf.at[each, part], sem.at[each])
                relays(each)[part].start()

    def rates(dy):
        source = (y + 4 - dy) % 4
        arrived(r_buf.at[rows_of(source, 4)], r_in.at[source])

    def updates(dy, other):
        block = ((y + 4 - dy) % 4) * 2 + (z // 2 + other) % 2
        for head in range(2):
            update(block, head, k_buf, v_buf, r_buf, w_ref, u_buf)

    forward(0, 0)
    u_buf[...] = jnp.zeros_like(u_buf)
    for source in range(4):
        arrived(rt_buf.at[source], rt_in.at[source])
    for dy in TURNS:
        r_relay(dy).start()
    pltpu.make_async_copy(rt_buf.at[:, y], r_buf.at[rows_of(y, 4)], r_in.at[y]).start()
    relay(0, 1)
    forward(1, 0)
    forward(3, 0)
    relay(2, 3)
    forward(2, 0)
    relay(4, 5)
    forward(1, -1)
    forward(3, -1)
    forward(1, 1)
    forward(3, 1)
    forward(0, -1)
    forward(0, 1)
    for slot in range(6, len(SLOTS)):
        for copy in slot_sends(slot):
            copy.start()
    for copy in kv_sends(straight[5]):
        copy.start()
    weights.wait()
    for dy in range(4):
        rates(dy)
    updates(0, 0)
    updates(1, 0)
    relay(6)
    updates(3, 0)
    forward(2, -1)
    forward(2, 1)
    relay(7)
    updates(2, 0)
    relay(8)
    pltpu.make_async_copy(columns(q_hbm, me), q_buf.at[mine], q_in.at[me]).start()
    for peer in near_peers:
        q_send(peer).start()
    forward(1, 2)
    updates(1, 1)
    forward(3, 2)
    updates(3, 1)
    forward(0, 2)
    updates(0, 1)
    forward(2, 2)
    for peer in far_peers:
        q_send(peer).start()
    updates(2, 1)

    def u_send(line):
        return remote(ub_buf.at[line], u_in.at[ctx], u_sent.at[line], u_got.at[ctx], (line, me))

    def p_send(line):
        return remote(p_out.at[line], p_buf.at[rows_of(ctx, SLICE)], p_sent.at[line], p_got.at[ctx], (line, me))

    for line in range(CTX):
        ub_buf[line] = u_buf[pl.ds(line * SLICE, SLICE), :].astype(BF16)
    for line in lines:
        u_send(line).start()
    u_in[ctx] = ub_buf[ctx]

    @pl.loop(0, PEERS)
    def _(source):
        early = rows_of(source, ROWS)
        arrived(k_buf.at[early], fk_in.at[source])
        arrived(v_buf.at[early], fv_in.at[source])

    def o_send(source):
        here = rows_of(source, ROWS)
        return remote(
            o_buf.at[here], columns(out_hbm, me), o_sent.at[source], o_in.at[me], (ctx, source)
        )

    def o_local():
        return pltpu.make_async_copy(o_buf.at[mine], columns(out_hbm, me), o_in.at[me])

    def o_slot(dy, dz):
        return (dz - 1) * 3 + dy - 1

    def o_aside(source, slot):
        there = o_in_slot.at[slot]
        here = rows_of(source, ROWS)
        return remote(o_buf.at[here], there, ot_sent.at[slot], ot_in.at[slot], (ctx, y * 4 + source % 4))

    def o_relay(dy, from_z, slot):
        there = columns(out_hbm, y * 4 + from_z)
        peer = ((y + dy) % 4) * 4 + z
        return remote(o_in_slot.at[slot], there, oa_sent.at[slot], o_in.at[y * 4 + from_z], (ctx, peer))

    def finish(step):
        back, _ = turn_at(step)
        dy = (4 - back) % 4
        block = block_at(step)
        for head in range(2):
            recall(block, head, q_buf, f_buf, a_buf, o_buf)
        for half in range(2):
            source = 2 * block + half
            dz = (source + 4 - z) % 4

            @pl.when(source == me)
            def _():
                o_local().start()

            @pl.when(jnp.logical_and(source != me, dy * dz == 0))
            def _():
                o_send(source).start()

            @pl.when(dy * dz != 0)
            def _():
                o_aside(source, o_slot(dy, dz)).start()

    def pass_on(step):
        back, other = turn_at(step)
        dy = (4 - back) % 4
        for half in range(2):
            from_z = 2 * ((z // 2 + other) % 2) + half
            dz = (z + 4 - from_z) % 4

            @pl.when(dy * dz != 0)
            def _():
                slot = o_slot(dy, dz)
                arrived(o_in_slot.at[slot], ot_in.at[slot])
                o_relay(dy, from_z, slot).start()

    @pl.loop(0, BLOCKS)
    def _(step):
        block = block_at(step)
        for half in range(2):
            source = 2 * block + half
            arrived(q_buf.at[rows_of(source, ROWS)], q_in.at[source])
        for head in range(2):
            attend(block, head, first, q_buf, k_buf, v_buf, s_buf, a_buf)

        @pl.when(step == SUM_STEP)
        def _():
            for line in lines:
                arrived(u_in.at[line], u_got.at[line])
            running = jnp.zeros((SLICE, HD), F32)
            for line in range(CTX):
                p_out[line] = running.astype(BF16)
                running = running + u_in[line].astype(F32)
            for line in lines:
                p_send(line).start()
            p_buf[rows_of(ctx, SLICE), :] = p_out[ctx]

        @pl.when(step == FIT_STEP)
        def _():
            for line in lines:
                arrived(p_buf.at[rows_of(line, SLICE)], p_got.at[line])
            for part in range(3):
                fit(part, w_ref, p_buf, f_buf)

            @pl.loop(0, FIT_STEP)
            def _(past):
                finish(past)

        @pl.when(step >= FIT_STEP)
        def _():
            finish(step)

        @pl.when(step > FIT_STEP)
        def _():
            pass_on(step - FIT_STEP - 1)

    @pl.loop(BLOCKS - FIT_STEP - 1, BLOCKS - 2)
    def _(step):
        pass_on(step)

    for turn in TURNS:
        r_aside(turn).wait_send()
        r_relay(turn).wait_send()
    for peer in straight:
        for copy in kv_sends(peer):
            copy.wait_send()
    for slot in range(len(SLOTS)):
        for copy in slot_sends(slot) + relays(slot):
            copy.wait_send()
    for peer in peers:
        q_send(peer).wait_send()
    for line in lines:
        u_send(line).wait_send()
        p_send(line).wait_send()

    @pl.loop(0, PEERS)
    def _(source):
        for copy in forwards(source):
            copy.wait_send()

    for peer in straight:
        o_send(peer).wait_send()
    for dy, dz in OFFSETS:
        if dy * dz:
            slot = o_slot(dy, dz)
            o_aside(device_at(dy, dz), slot).wait_send()
            o_relay(dy, (z + 4 - dz) % 4, slot).wait_send()
    for peer in peers:
        arrived(columns(out_hbm, peer), o_in.at[peer])
    arrived(columns(out_hbm, me), o_in.at[me])


def norm_kernel(x_ref, gain_ref, out_ref):
    wide = x_ref[...].astype(F32)
    factor = lax.rsqrt(jnp.mean(wide * wide, axis=1, keepdims=True) + EPSILON)
    out_ref[...] = (wide * factor * gain_ref[...]).astype(BF16)


def on_device(queries, keys, values, rates, fast_init, gain):
    rate_rows = rates.T.reshape(4, 4, 2, ROWS)
    anywhere = pl.BlockSpec(memory_space=pl.ANY)
    dma = pltpu.SemaphoreType.DMA
    wide = pl.pallas_call(
        main_kernel,
        out_shape=jax.ShapeDtypeStruct((ROWS, PEERS * COLS), BF16),
        in_specs=[anywhere] * 5,
        out_specs=anywhere,
        scratch_shapes=[
            pltpu.VMEM((3, 2, HD, HD), BF16),
            dma(()),
            pltpu.VMEM((GROUP, COLS), BF16),
            pltpu.VMEM((2 * GROUP, COLS), BF16),
            pltpu.VMEM((2 * GROUP, COLS), BF16),
            pltpu.VMEM((len(SLOTS), 2, ROWS, COLS), BF16),
            pltpu.VMEM((4, 4, 2, ROWS), BF16),
            pltpu.VMEM((PEERS, 2, ROWS), BF16),
            pltpu.VMEM((2, BLOCK, GROUP), F32),
            pltpu.VMEM((GROUP, COLS), F32),
            pltpu.VMEM((GROUP, COLS), BF16),
            pltpu.VMEM((len(SLOTS), ROWS, COLS), BF16),
            pltpu.VMEM((6 * HD, HD), F32),
            pltpu.VMEM((CTX, SLICE, HD), BF16),
            pltpu.VMEM((CTX, SLICE, HD), BF16),
            pltpu.VMEM((CTX, SLICE, HD), BF16),
            pltpu.VMEM((6 * HD, HD), BF16),
            pltpu.VMEM((6, HD, HD), BF16),
        ]
        + [dma((PEERS,))] * 8
        + [dma((4,))] * 4
        + [dma((PEERS,))] * 4
        + [dma((len(SLOTS),))] * 9
        + [dma((CTX,))] * 4,
        compiler_params=pltpu.CompilerParams(
            collective_id=0, has_side_effects=True, vmem_limit_bytes=67_043_328
        ),
        name="layer",
    )(queries, keys, values, rate_rows, fast_init)
    tile = 64
    return pl.pallas_call(
        norm_kernel,
        grid=(ROWS // tile,),
        out_shape=jax.ShapeDtypeStruct((ROWS, PEERS * COLS), BF16),
        in_specs=[
            pl.BlockSpec((tile, PEERS * COLS), lambda i: (i, 0)),
            pl.BlockSpec((1, PEERS * COLS), lambda i: (0, 0)),
        ],
        out_specs=pl.BlockSpec((tile, PEERS * COLS), lambda i: (i, 0)),
        name="norm",
    )(wide, gain.reshape(1, -1))


def solution(mesh):
    rows = P(("ctx", "head"), None)
    return jax.shard_map(
        on_device,
        mesh=mesh,
        in_specs=(rows, rows, rows, rows, P(None, "head", None, None), P()),
        out_specs=rows,
        check_vma=False,
    )
```

```python
import functools

import jax
import jax.numpy as jnp
from jax import lax
from jax.experimental import pallas as pl
from jax.experimental.pallas import tpu as pltpu
from jax.sharding import PartitionSpec as P

F32 = jnp.float32
BF16 = jnp.bfloat16
MESH = pl.DeviceIdType.MESH
EPSILON = 1e-06
NT = (((1,), (1,)), ((), ()))
NN = (((1,), (0,)), ((), ()))
TN = (((0,), (0,)), ((), ()))

CTX = 8
PEERS = 16
GROUP = 2048
ROWS = 128
COLS = 512
HD = 256
BLOCK = 256
BLOCKS = GROUP // BLOCK
SLICE = 6 * HD // CTX
SCALE = HD**-0.5 * 1.4426950408889634
LOW = -1e30
SUM_STEP = 0
FIT_STEP = 2

TURNS = (1, 3, 2)

OFFSETS = (
    (0, 1), (1, 0), (0, 3), (3, 0), (1, 1), (3, 3), (1, 3), (3, 1),
    (0, 2), (2, 0), (1, 2), (2, 1), (3, 2), (2, 3), (2, 2),
)
FAR = ((1, 1), (3, 3), (1, 3), (3, 1), (0, 2), (1, 2), (3, 2), (2, 0), (2, 1), (2, 3), (2, 2))
SLOTS = ((1, 1), (3, 1), (1, 3), (3, 3), (1, 2), (3, 2), (2, 1), (2, 3), (2, 2))


def dot(a, b, dims):
    return lax.dot_general(a, b, dims, preferred_element_type=F32)


def rows_of(index, size, base=0):
    return pl.ds(pl.multiple_of(base + index * size, size), size)


def head_columns(head):
    return slice(head * HD, head * HD + HD)


def attend(block, head, first, q_buf, k_buf, v_buf, s_buf, a_buf):
    cols = head_columns(head)
    here = rows_of(block, BLOCK)
    query = q_buf[here, cols]
    lane = lax.broadcasted_iota(jnp.int32, (BLOCK, HD), 1)
    row = lax.broadcasted_iota(jnp.int32, (BLOCK, HD), 0)
    far = lane > row

    def bias(tile):
        return jnp.where(jnp.logical_and(first, block + tile < BLOCKS), LOW, 0.0).astype(F32)

    def keys(tile):
        return k_buf[rows_of(block + tile, BLOCK), cols]

    def values(tile):
        return v_buf[rows_of(block + tile, BLOCK), cols]

    score = jnp.where(far, dot(query, keys(0), NT) + bias(0), dot(query, keys(BLOCKS), NT))
    s_buf[head, :, 0:HD] = score
    top = jnp.maximum(score[:, :128], score[:, 128:])
    for tile in range(1, BLOCKS):
        score = dot(query, keys(tile), NT)
        s_buf[head, :, tile * HD : tile * HD + HD] = score
        top = jnp.maximum(top, jnp.maximum(score[:, :128], score[:, 128:]) + bias(tile))
    top = jnp.max(top, axis=1, keepdims=True) * SCALE
    prob = jnp.exp2(s_buf[head, :, 0:HD] * SCALE - top)
    total = prob[:, :128] + prob[:, 128:]
    out = dot(jnp.where(far, prob, 0.0).astype(BF16), values(0), NN)
    out = out + dot(jnp.where(far, 0.0, prob).astype(BF16), values(BLOCKS), NN)
    for tile in range(1, BLOCKS):
        prob = jnp.exp2(s_buf[head, :, tile * HD : tile * HD + HD] * SCALE + (bias(tile) * SCALE - top))
        total = total + (prob[:, :128] + prob[:, 128:])
        out = out + dot(prob.astype(BF16), values(tile), NN)
    a_buf[here, cols] = out / jnp.sum(total, axis=1, keepdims=True)


def recall(block, head, q_buf, f_buf, a_buf, o_buf):
    cols = head_columns(head)
    here = rows_of(block, BLOCK)
    query = q_buf[here, cols]
    gate = dot(query, f_buf[head], NT)
    up = dot(query, f_buf[2 + head], NT)
    hidden = (gate * jax.nn.sigmoid(gate) * up).astype(BF16)
    o_buf[here, cols] = (a_buf[here, cols] + dot(hidden, f_buf[4 + head], NN)).astype(BF16)


def update(block, head, k_buf, v_buf, r_buf, w_ref, u_buf):
    cols = head_columns(head)
    here = rows_of(block, BLOCK, GROUP)
    key = k_buf[here, cols]
    value = v_buf[here, cols]
    lines = [r_buf[2 * block + half].astype(F32)[head : head + 1] for half in range(2)]
    rate = jnp.concatenate([jnp.broadcast_to(line, (8, ROWS)).T for line in lines], 0)[:, :1]
    target = (rate * value.astype(F32)).astype(BF16)
    gate = dot(key, w_ref[0, head], NT)
    up = dot(key, w_ref[1, head], NT)
    back = dot(target, w_ref[2, head], NT)
    sigma = jax.nn.sigmoid(gate)
    act = gate * sigma
    hidden = (act * up).astype(BF16)
    back_gate = (back * up * sigma * (1.0 + gate * (1.0 - sigma))).astype(BF16)
    back_up = (back * act).astype(BF16)
    for part, left, right in ((0, back_gate, key), (1, back_up, key), (2, hidden, target)):
        place = pl.ds((2 * part + head) * HD, HD)
        u_buf[place, :] += dot(left, right, TN)


def fit(part, w_ref, p_buf, f_buf):
    for head in range(2):
        initial = w_ref[part, head].astype(F32)
        renewed = initial + p_buf[pl.ds((2 * part + head) * HD, HD), :].astype(F32)
        wanted = jnp.mean(initial * initial, axis=1, keepdims=True)
        current = jnp.mean(renewed * renewed, axis=1, keepdims=True)
        f_buf[2 * part + head] = (renewed * jnp.sqrt(wanted) * lax.rsqrt(current + EPSILON)).astype(BF16)


def main_kernel(
    q_hbm, k_hbm, v_hbm, r_hbm, w_hbm, out_hbm,
    w_ref, w_in,
    q_buf, k_buf, v_buf, t_buf, rt_buf, r_buf, s_buf, a_buf, o_buf, o_in_slot, u_buf, ub_buf, u_in, p_out, p_buf, f_buf,
    q_in, k_in, v_in, o_in, q_sent, k_sent, v_sent, o_sent, rt_in, rt_sent, r_in, r_sent,
    fk_in, fv_in, fk_sent, fv_sent, t_in, tv_in, tk_sent, tv_sent, ak_sent, av_sent, ot_in, ot_sent, oa_sent, u_got, u_sent, p_got, p_sent,
):
    ctx = lax.axis_index("ctx")
    me = lax.axis_index("head")
    y, z = me // 4, me % 4
    first = ctx == 0
    after = (ctx + 1) % CTX
    peers = [((y + dy) % 4) * 4 + (z + dz) % 4 for dy, dz in OFFSETS]
    lines = [(ctx + step) % CTX for step in range(1, CTX)]

    barrier = pltpu.get_barrier_semaphore()
    for peer in peers:
        pl.semaphore_signal(barrier, inc=1, device_id=(ctx, peer), device_id_type=MESH)
    for line in lines:
        pl.semaphore_signal(barrier, inc=1, device_id=(line, me), device_id_type=MESH)
    weights = pltpu.make_async_copy(w_hbm, w_ref, w_in)
    weights.start()
    pl.semaphore_wait(barrier, len(peers) + len(lines))

    def remote(src, dst, sent, got, where):
        return pltpu.make_async_remote_copy(
            src_ref=src, dst_ref=dst, send_sem=sent, recv_sem=got, device_id=where, device_id_type=MESH
        )

    def columns(ref, peer):
        return ref.at[:, pl.ds(pl.multiple_of(peer * COLS, COLS), COLS)]

    mine = rows_of(me, ROWS)
    mine_late = rows_of(me, ROWS, GROUP)

    def device_at(dy, dz):
        return ((y + dy + 4) % 4) * 4 + (z + dz + 4) % 4

    def kv_sends(peer):
        return (
            remote(columns(k_hbm, peer), k_buf.at[mine_late], k_sent.at[peer], k_in.at[me], (ctx, peer)),
            remote(columns(v_hbm, peer), v_buf.at[mine_late], v_sent.at[peer], v_in.at[me], (ctx, peer)),
        )

    def r_aside(dz):
        way = (z + dz) % 4
        return remote(r_hbm.at[:, way], rt_buf.at[z], rt_sent.at[dz], rt_in.at[z], (ctx, y * 4 + way))

    def r_relay(dy):
        way = (y + dy) % 4
        return remote(rt_buf.at[:, way], r_buf.at[rows_of(y, 4)], r_sent.at[dy], r_in.at[y], (ctx, way * 4 + z))

    def slot_sends(slot):
        dz, dy = SLOTS[slot]
        peer, way = device_at(dy, dz), device_at(0, dz)
        return (
            remote(columns(k_hbm, peer), t_buf.at[slot, 0], tk_sent.at[slot], t_in.at[slot], (ctx, way)),
            remote(columns(v_hbm, peer), t_buf.at[slot, 1], tv_sent.at[slot], tv_in.at[slot], (ctx, way)),
        )

    def relays(slot):
        dz, dy = SLOTS[slot]
        source, peer = device_at(0, -dz), device_at(dy, 0)
        there = rows_of(source, ROWS, GROUP)
        return (
            remote(t_buf.at[slot, 0], k_buf.at[there], ak_sent.at[slot], k_in.at[source], (ctx, peer)),
            remote(t_buf.at[slot, 1], v_buf.at[there], av_sent.at[slot], v_in.at[source], (ctx, peer)),
        )

    def q_send(peer):
        return remote(columns(q_hbm, peer), q_buf.at[mine], q_sent.at[peer], q_in.at[me], (ctx, peer))

    pltpu.make_async_copy(columns(k_hbm, me), k_buf.at[mine_late], k_in.at[me]).start()
    pltpu.make_async_copy(columns(v_hbm, me), v_buf.at[mine_late], v_in.at[me]).start()
    pltpu.make_async_copy(r_hbm.at[:, z], rt_buf.at[z], rt_in.at[z]).start()
    for dz in TURNS:
        r_aside(dz).start()
    straight = [device_at(dy, 0) for dy in TURNS] + [device_at(0, dz) for dz in TURNS]
    for peer in straight[:3]:
        for copy in kv_sends(peer):
            copy.start()
    for slot in range(6):
        for copy in slot_sends(slot):
            copy.start()
    for peer in straight[3:5]:
        for copy in kv_sends(peer):
            copy.start()

    def arrived(ref, sem):
        pltpu.make_async_copy(ref, ref, sem).wait()

    def turn_at(step):
        last = step // 6
        far = step // 4 - last
        near = 1 - far - last
        dy = near * (1 + 2 * (step % 2)) + 2 * far
        return dy, near * (step // 2) + far * (step % 2) + last * (1 - step % 2)

    def block_at(step):
        dy, other = turn_at(step)
        return ((y + 4 - dy) % 4) * 2 + (z // 2 + other) % 2

    near_peers = [device_at(*turn) for turn in ((1, 0), (3, 0), (0, 1), (0, 3))]
    far_peers = [device_at(*turn) for turn in FAR]

    def forwards(source):
        late, early = rows_of(source, ROWS, GROUP), rows_of(source, ROWS)
        return (
            remote(k_buf.at[late], k_buf.at[early], fk_sent.at[source], fk_in.at[source], (after, me)),
            remote(v_buf.at[late], v_buf.at[early], fv_sent.at[source], fv_in.at[source], (after, me)),
        )

    def forward(dy, dz):
        source = device_at(-dy, dz)
        late = rows_of(source, ROWS, GROUP)
        arrived(k_buf.at[late], k_in.at[source])
        arrived(v_buf.at[late], v_in.at[source])
        for copy in forwards(source):
            copy.start()

    def relay(slot, *more):
        for part, sem in ((0, t_in), (1, tv_in)):
            for each in (slot,) + more:
                arrived(t_buf.at[each, part], sem.at[each])
                relays(each)[part].start()

    def rates(dy):
        source = (y + 4 - dy) % 4
        arrived(r_buf.at[rows_of(source, 4)], r_in.at[source])

    def updates(dy, other):
        block = ((y + 4 - dy) % 4) * 2 + (z // 2 + other) % 2
        for head in range(2):
            update(block, head, k_buf, v_buf, r_buf, w_ref, u_buf)

    forward(0, 0)
    u_buf[...] = jnp.zeros_like(u_buf)
    for source in range(4):
        arrived(rt_buf.at[source], rt_in.at[source])
    for dy in TURNS:
        r_relay(dy).start()
    pltpu.make_async_copy(rt_buf.at[:, y], r_buf.at[rows_of(y, 4)], r_in.at[y]).start()
    relay(0, 1)
    forward(1, 0)
    forward(3, 0)
    relay(2, 3)
    forward(2, 0)
    relay(4, 5)
    forward(1, -1)
    forward(3, -1)
    forward(1, 1)
    forward(3, 1)
    forward(0, -1)
    forward(0, 1)
    for slot in range(6, len(SLOTS)):
        for copy in slot_sends(slot):
            copy.start()
    for copy in kv_sends(straight[5]):
        copy.start()
    weights.wait()
    for dy in range(4):
        rates(dy)
    updates(0, 0)
    updates(1, 0)
    relay(6)
    updates(3, 0)
    forward(2, -1)
    forward(2, 1)
    relay(7)
    updates(2, 0)
    relay(8)
    pltpu.make_async_copy(columns(q_hbm, me), q_buf.at[mine], q_in.at[me]).start()
    for peer in near_peers:
        q_send(peer).start()
    forward(1, 2)
    updates(1, 1)
    forward(3, 2)
    updates(3, 1)
    forward(0, 2)
    updates(0, 1)
    forward(2, 2)
    for peer in far_peers:
        q_send(peer).start()
    updates(2, 1)

    def u_send(line):
        return remote(ub_buf.at[line], u_in.at[ctx], u_sent.at[line], u_got.at[ctx], (line, me))

    def p_send(line):
        return remote(p_out.at[line], p_buf.at[rows_of(ctx, SLICE)], p_sent.at[line], p_got.at[ctx], (line, me))

    for line in range(CTX):
        ub_buf[line] = u_buf[pl.ds(line * SLICE, SLICE), :].astype(BF16)
    for line in lines:
        u_send(line).start()
    u_in[ctx] = ub_buf[ctx]

    @pl.loop(0, PEERS)
    def _(source):
        early = rows_of(source, ROWS)
        arrived(k_buf.at[early], fk_in.at[source])
        arrived(v_buf.at[early], fv_in.at[source])

    def o_send(source):
        here = rows_of(source, ROWS)
        return remote(
            o_buf.at[here], columns(out_hbm, me), o_sent.at[source], o_in.at[me], (ctx, source)
        )

    def o_local():
        return pltpu.make_async_copy(o_buf.at[mine], columns(out_hbm, me), o_in.at[me])

    def o_slot(dy, dz):
        return (dz - 1) * 3 + dy - 1

    def o_aside(source, slot):
        there = o_in_slot.at[slot]
        here = rows_of(source, ROWS)
        return remote(o_buf.at[here], there, ot_sent.at[slot], ot_in.at[slot], (ctx, y * 4 + source % 4))

    def o_relay(dy, from_z, slot):
        there = columns(out_hbm, y * 4 + from_z)
        peer = ((y + dy) % 4) * 4 + z
        return remote(o_in_slot.at[slot], there, oa_sent.at[slot], o_in.at[y * 4 + from_z], (ctx, peer))

    def finish(step):
        back, _ = turn_at(step)
        dy = (4 - back) % 4
        block = block_at(step)
        for head in range(2):
            recall(block, head, q_buf, f_buf, a_buf, o_buf)
        for half in range(2):
            source = 2 * block + half
            dz = (source + 4 - z) % 4

            @pl.when(source == me)
            def _():
                o_local().start()

            @pl.when(jnp.logical_and(source != me, dy * dz == 0))
            def _():
                o_send(source).start()

            @pl.when(dy * dz != 0)
            def _():
                o_aside(source, o_slot(dy, dz)).start()

    def pass_on(step):
        back, other = turn_at(step)
        dy = (4 - back) % 4
        for half in range(2):
            from_z = 2 * ((z // 2 + other) % 2) + half
            dz = (z + 4 - from_z) % 4

            @pl.when(dy * dz != 0)
            def _():
                slot = o_slot(dy, dz)
                arrived(o_in_slot.at[slot], ot_in.at[slot])
                o_relay(dy, from_z, slot).start()

    @pl.loop(0, BLOCKS)
    def _(step):
        block = block_at(step)
        for half in range(2):
            source = 2 * block + half
            arrived(q_buf.at[rows_of(source, ROWS)], q_in.at[source])
        for head in range(2):
            attend(block, head, first, q_buf, k_buf, v_buf, s_buf, a_buf)

        @pl.when(step == SUM_STEP)
        def _():
            for line in lines:
                arrived(u_in.at[line], u_got.at[line])
            running = jnp.zeros((SLICE, HD), F32)
            for line in range(CTX):
                p_out[line] = running.astype(BF16)
                running = running + u_in[line].astype(F32)
            for line in lines:
                p_send(line).start()
            p_buf[rows_of(ctx, SLICE), :] = p_out[ctx]

        @pl.when(step == FIT_STEP)
        def _():
            for line in lines:
                arrived(p_buf.at[rows_of(line, SLICE)], p_got.at[line])
            for part in range(3):
                fit(part, w_ref, p_buf, f_buf)

            @pl.loop(0, FIT_STEP)
            def _(past):
                finish(past)

        @pl.when(step >= FIT_STEP)
        def _():
            finish(step)

        @pl.when(step > FIT_STEP)
        def _():
            pass_on(step - FIT_STEP - 1)

    @pl.loop(BLOCKS - FIT_STEP - 1, BLOCKS - 2)
    def _(step):
        pass_on(step)

    for turn in TURNS:
        r_aside(turn).wait_send()
        r_relay(turn).wait_send()
    for peer in straight:
        for copy in kv_sends(peer):
            copy.wait_send()
    for slot in range(len(SLOTS)):
        for copy in slot_sends(slot) + relays(slot):
            copy.wait_send()
    for peer in peers:
        q_send(peer).wait_send()
    for line in lines:
        u_send(line).wait_send()
        p_send(line).wait_send()

    @pl.loop(0, PEERS)
    def _(source):
        for copy in forwards(source):
            copy.wait_send()

    for peer in straight:
        o_send(peer).wait_send()
    for dy, dz in OFFSETS:
        if dy * dz:
            slot = o_slot(dy, dz)
            o_aside(device_at(dy, dz), slot).wait_send()
            o_relay(dy, (z + 4 - dz) % 4, slot).wait_send()
    for peer in peers:
        arrived(columns(out_hbm, peer), o_in.at[peer])
    arrived(columns(out_hbm, me), o_in.at[me])


def norm_kernel(x_ref, gain_ref, out_ref):
    strip, lanes = 16, 128
    for top in range(0, x_ref.shape[0], strip):
        rows = slice(top, top + strip)
        squares = jnp.zeros((strip, lanes), F32)
        for left in range(0, x_ref.shape[1], lanes):
            part = x_ref[rows, left : left + lanes].astype(F32)
            squares = squares + part * part
        mean = jnp.sum(squares, axis=1, keepdims=True) / x_ref.shape[1]
        factor = lax.rsqrt(mean + EPSILON)
        for left in range(0, x_ref.shape[1], lanes):
            cols = slice(left, left + lanes)
            out_ref[rows, cols] = (x_ref[rows, cols].astype(F32) * factor * gain_ref[:, cols]).astype(BF16)


def on_device(queries, keys, values, rates, fast_init, gain):
    rate_rows = rates.T.reshape(4, 4, 2, ROWS)
    anywhere = pl.BlockSpec(memory_space=pl.ANY)
    dma = pltpu.SemaphoreType.DMA
    wide = pl.pallas_call(
        main_kernel,
        out_shape=jax.ShapeDtypeStruct((ROWS, PEERS * COLS), BF16),
        in_specs=[anywhere] * 5,
        out_specs=anywhere,
        scratch_shapes=[
            pltpu.VMEM((3, 2, HD, HD), BF16),
            dma(()),
            pltpu.VMEM((GROUP, COLS), BF16),
            pltpu.VMEM((2 * GROUP, COLS), BF16),
            pltpu.VMEM((2 * GROUP, COLS), BF16),
            pltpu.VMEM((len(SLOTS), 2, ROWS, COLS), BF16),
            pltpu.VMEM((4, 4, 2, ROWS), BF16),
            pltpu.VMEM((PEERS, 2, ROWS), BF16),
            pltpu.VMEM((2, BLOCK, GROUP), F32),
            pltpu.VMEM((GROUP, COLS), F32),
            pltpu.VMEM((GROUP, COLS), BF16),
            pltpu.VMEM((len(SLOTS), ROWS, COLS), BF16),
            pltpu.VMEM((6 * HD, HD), F32),
            pltpu.VMEM((CTX, SLICE, HD), BF16),
            pltpu.VMEM((CTX, SLICE, HD), BF16),
            pltpu.VMEM((CTX, SLICE, HD), BF16),
            pltpu.VMEM((6 * HD, HD), BF16),
            pltpu.VMEM((6, HD, HD), BF16),
        ]
        + [dma((PEERS,))] * 8
        + [dma((4,))] * 4
        + [dma((PEERS,))] * 4
        + [dma((len(SLOTS),))] * 9
        + [dma((CTX,))] * 4,
        compiler_params=pltpu.CompilerParams(
            collective_id=0, has_side_effects=True, vmem_limit_bytes=67_043_328
        ),
        name="layer",
    )(queries, keys, values, rate_rows, fast_init)
    tile = 64
    return pl.pallas_call(
        norm_kernel,
        grid=(ROWS // tile,),
        out_shape=jax.ShapeDtypeStruct((ROWS, PEERS * COLS), BF16),
        in_specs=[
            pl.BlockSpec((tile, PEERS * COLS), lambda i: (i, 0)),
            pl.BlockSpec((1, PEERS * COLS), lambda i: (0, 0)),
        ],
        out_specs=pl.BlockSpec((tile, PEERS * COLS), lambda i: (i, 0)),
        name="norm",
    )(wide, gain.reshape(1, -1))


def solution(mesh):
    rows = P(("ctx", "head"), None)
    return jax.shard_map(
        on_device,
        mesh=mesh,
        in_specs=(rows, rows, rows, rows, P(None, "head", None, None), P()),
        out_specs=rows,
        check_vma=False,
    )
```
